1024 devices in a mesh: wide: 64 (over y, z_lo, core), narrow: 16 (over x, z_hi).
Axes of the slice: x: 4, y: 4, z: 32 (z_hi: 4, z_lo: 8; z = z_hi * 8 + z_lo), core: 2. Of those that a mesh axis runs over, the one named last changes fastest.
Arguments:
- kirchhoff: float32 [256, 512, 512], P('wide', 'narrow'), may hold values from -24 to 24
- adjoint: float32 [256, 512, 512], P('wide', 'narrow'), may hold values from -24 to 24
- penalty_slope: bfloat16 [256, 512, 512], P('wide', 'narrow'), may hold values from 0.29882812 to 3
- design: float32 [256, 128, 256], P('narrow', 'wide'), may hold values from 0 to 1
- solid_mask: int32 [256, 128, 256], P('narrow', 'wide'), may hold values 0 or 1
- void_mask: int32 [256, 128, 256], P('narrow', 'wide'), may hold values 0 or 1
Outputs:
- projected_density: float32 [256, 128, 256], P('narrow', 'wide')
- design_sens: float32 [256, 128, 256], P('narrow', 'wide')
The draws below stay inside these ranges and needn't reach their ends.
All inputs are finite; a program needn't handle non-finite values. No bound on the sum of `solid_mask` or of `void_mask` on one device may be relied on, other than what follows from the above.
Results may differ from the reference program's by a relative error of at most 0.0003.
Values sent between devices are 32-bit elements; how exact they have to be, the bound alone decides.
No kernel may reach another device: no remote copies, remote signals or barrier semaphores. Data moves between devices by JAX's collectives and lax.ppermute only.
A program may use at most 64 MiB of HBM per device.

```python
import math
import jax
import jax.numpy as jnp
from jax import lax

AZ = 512
RADIUS = 12
AX = 256
AY = 512
DX = 128
DY = 256
DZ = 256


def set_ends(drawn, key, least, top_value):
    index_at = [jax.random.randint(jax.random.fold_in(key, axis), (), 0, length) for axis, length in enumerate(drawn.shape)]
    longest = drawn.shape.index(max(drawn.shape))
    neighbour = index_at[:longest] + [(index_at[longest] + 1) % drawn.shape[longest]] + index_at[longest + 1:]
    return drawn.at[tuple(index_at)].set(least).at[tuple(neighbour)].set(top_value)


def block_levels(stream_key, shape, cuts, smallest, top_value):
    factor_of = 1.0
    for dim, shards_of in cuts:
        steps = jax.random.uniform(jax.random.fold_in(jax.random.fold_in(stream_key, 6), dim), (shards_of,), jnp.float32, smallest / len(cuts), top_value / len(cuts))
        factor_of = factor_of * jnp.repeat(jnp.exp(steps), shape[dim] // shards_of).reshape((-1,) + (1,) * (len(shape) - 1 - dim))
    return factor_of


def noise(stream_key, shape, scale, limit, shards=(), kind=jnp.bfloat16):
    factor_of = block_levels(stream_key, shape, shards, -0.22, 0.18) if shards else 1.0
    entries = jax.random.normal(stream_key, shape, jnp.float32) * scale * factor_of
    return jnp.minimum(jnp.maximum(entries, -limit), limit).astype(kind)


def setup_inputs(seed: int = 0) -> dict:
    arg_keys = jax.random.split(jax.random.key(seed), 7)
    return {
        "kirchhoff": noise(arg_keys[0], (AX, AY, AZ), 4.0, 24.0, ((0, 64), (1, 16)), jnp.float32),
        "adjoint": noise(arg_keys[1], (AX, AY, AZ), 4.0, 24.0, ((0, 64), (1, 16)), jnp.float32),
        "penalty_slope": jnp.clip(jnp.exp(math.log(3.0) - 2.306499 * jax.random.uniform(arg_keys[2], (AX, AY, AZ), jnp.float32) ** block_levels(arg_keys[2], (AX, AY, AZ), ((0, 64), (1, 16)), -0.2, 0.2)), 0.29882812, 3.0).astype(jnp.bfloat16),
        "design": jnp.clip(1.0 * jax.random.uniform(arg_keys[3], (DZ, DX, DY), jnp.float32) ** block_levels(arg_keys[3], (DZ, DX, DY), ((0, 16), (1, 64)), -0.2, 0.2), 0.0, 1.0),
        "solid_mask": set_ends((jax.random.randint(arg_keys[4], (DZ, DX, DY), 0, 8) < 1).astype(jnp.int32), jax.random.fold_in(arg_keys[4], 1), 0, 1),
        "void_mask": set_ends((jax.random.randint(arg_keys[5], (DZ, DX, DY), 0, 8) < 1).astype(jnp.int32), jax.random.fold_in(arg_keys[5], 1), 0, 1),
    }


BETA = 32.0
ETA = 0.5
LOWER_TANH = math.tanh(BETA * ETA)
SPAN_TANH = math.tanh(BETA * ETA) + math.tanh(BETA * (1.0 - ETA))


def smooth_axis(values, dimension):
    extent = values.shape[dimension]
    widths = [(0, 0)] * values.ndim
    widths[dimension] = (RADIUS, RADIUS)
    padded = jnp.pad(values, widths)
    running = jnp.zeros_like(values)
    for offset in range(2 * RADIUS + 1):
        weight = float(RADIUS + 1 - abs(offset - RADIUS))
        running = running + weight * lax.slice_in_dim(padded, offset, offset + extent, axis=dimension)
    return running


def smooth(values):
    return smooth_axis(smooth_axis(smooth_axis(values, 2), 0), 1)


def cover(extent):
    return smooth_axis(jnp.ones((extent,), jnp.float32), 0)


def heaviside(values):
    return (LOWER_TANH + jnp.tanh(BETA * (values - ETA))) / SPAN_TANH


def heaviside_slope(values):
    inner = jnp.tanh(BETA * (values - ETA))
    return BETA * (1.0 - inner * inner) / SPAN_TANH


def restrict(ghosted, coeffs):
    grad_x = ghosted[:, 2:, 1:-1, 1:-1] - ghosted[:, :-2, 1:-1, 1:-1]
    grad_y = ghosted[:, 1:-1, 2:, 1:-1] - ghosted[:, 1:-1, :-2, 1:-1]
    grad_z = ghosted[:, 1:-1, 1:-1, 2:] - ghosted[:, 1:-1, 1:-1, :-2]
    product = grad_x[0] * grad_x[1] + grad_y[0] * grad_y[1] + grad_z[0] * grad_z[1]
    sensed = -0.25 * coeffs * product
    x_cells, y_cells, z_cells = sensed.shape
    return sensed.reshape(x_cells // 2, 2, y_cells // 2, 2, z_cells // 2, 2).sum(axis=(1, 3, 5))


def reference(kirchhoff, adjoint, penalty_slope, design, solid_mask, void_mask):
    fields = jnp.pad(jnp.stack([kirchhoff, adjoint]), ((0, 0), (1, 1), (1, 1), (1, 1)))
    slopes = penalty_slope.astype(jnp.float32)

    def coarse_plane(index):
        start = (2 * index).astype(jnp.int32)
        ghosted = lax.dynamic_slice_in_dim(fields, start, 4, 1)
        coeffs = lax.dynamic_slice_in_dim(slopes, start, 2, 0)
        return restrict(ghosted, coeffs)[0]

    coarse = lax.map(coarse_plane, jnp.arange(DX, dtype=jnp.int32))
    coarse = jnp.transpose(coarse, (2, 0, 1))
    normalizer = cover(DZ)[:, None, None] * cover(DX)[None, :, None] * cover(DY)[None, None, :]
    is_solid = solid_mask.astype(jnp.float32)
    is_void = void_mask.astype(jnp.float32)
    live = (1.0 - is_solid) * (1.0 - is_void)
    filtered = smooth(design) / normalizer
    projected = heaviside(filtered) * live + is_solid * (1.0 - is_void)
    weighted = heaviside_slope(filtered) * coarse * live / normalizer
    design_sens = smooth(weighted) * live
    return projected, design_sens
```

```python
import math

import jax
import jax.numpy as jnp
from jax import lax
from jax.sharding import PartitionSpec as P

RADIUS = 12
BETA = 32.0
ETA = 0.5
LOWER_TANH = math.tanh(BETA * ETA)
SPAN_TANH = math.tanh(BETA * ETA) + math.tanh(BETA * (1.0 - ETA))
HIGHEST = lax.Precision.HIGHEST


def neighbours(shard, axis, dim):
    count, length = lax.axis_size(axis), shard.shape[dim]
    up = [(i, i + 1) for i in range(count - 1)]
    down = [(j, i) for i, j in up]
    before = lax.ppermute(lax.slice_in_dim(shard, length - 1, length, axis=dim), axis, up)
    after = lax.ppermute(lax.slice_in_dim(shard, 0, 1, axis=dim), axis, down)
    return before, after


def restrict(fields, coeffs, x_sides, y_sides):
    padded = jnp.concatenate([x_sides[0], fields, x_sides[1]], axis=1)
    grad_x = padded[:, 2:] - padded[:, :-2]
    padded = jnp.concatenate([y_sides[0], fields, y_sides[1]], axis=2)
    grad_y = padded[:, :, 2:] - padded[:, :, :-2]
    padded = jnp.pad(fields, ((0, 0), (0, 0), (0, 0), (1, 1)))
    grad_z = padded[..., 2:] - padded[..., :-2]
    product = grad_x[0] * grad_x[1] + grad_y[0] * grad_y[1] + grad_z[0] * grad_z[1]
    sensed = -0.25 * coeffs * product
    x_cells, y_cells, z_cells = sensed.shape
    sensed = sensed.reshape(x_cells // 2, 2, y_cells, z_cells).sum(axis=1)
    rows = lax.broadcasted_iota(jnp.int32, (z_cells, z_cells // 2), 0)
    cols = lax.broadcasted_iota(jnp.int32, (z_cells, z_cells // 2), 1)
    pairs = (rows // 2 == cols).astype(jnp.float32)
    sensed = jnp.einsum("xyz,zk->xyk", sensed, pairs, precision=HIGHEST)
    return sensed.reshape(x_cells // 2, y_cells // 2, 2, z_cells // 2).sum(axis=2)


def band(extent):
    out_pos = lax.broadcasted_iota(jnp.int32, (extent, extent), 0)
    in_pos = lax.broadcasted_iota(jnp.int32, (extent, extent), 1)
    return jnp.maximum(RADIUS + 1 - jnp.abs(in_pos - out_pos), 0).astype(jnp.float32)


def cover(positions, extent):
    low = jnp.maximum(RADIUS - positions, 0)
    high = jnp.maximum(RADIUS - (extent - 1 - positions), 0)
    total = (RADIUS + 1) ** 2
    return (total - low * (low + 1) // 2 - high * (high + 1) // 2).astype(jnp.float32)


def per_device(kirchhoff, adjoint, penalty_slope, design, solid_mask, void_mask):
    wide, narrow = lax.axis_size("wide"), lax.axis_size("narrow")
    zc, xc, y_all = design.shape
    z_all, x_all = zc * narrow, xc * wide
    yc, zw = y_all // narrow, z_all // wide

    is_solid = solid_mask.astype(jnp.float32)
    is_void = void_mask.astype(jnp.float32)
    live = (1.0 - is_solid) * (1.0 - is_void)

    along_y = jnp.einsum("zxj,ij->zxi", design, band(y_all), precision=HIGHEST)
    sent = jnp.stack([along_y, live], axis=1).reshape(zc, 2, xc, narrow, yc)
    sent = sent.transpose(3, 0, 1, 2, 4).reshape(narrow, 1, -1)
    got = lax.all_to_all(sent, "narrow", split_axis=0, concat_axis=0, tiled=True)
    got = got.reshape(z_all, 2, xc, yc)
    along_z = jnp.einsum("kz,zxy->kxy", band(z_all), got[:, 0], precision=HIGHEST)

    fields = jnp.stack([kirchhoff, adjoint])
    y_sides = neighbours(fields, "narrow", 2)
    x_sides = neighbours(fields, "wide", 1)
    coarse = restrict(fields, penalty_slope.astype(jnp.float32), x_sides, y_sides)
    coarse = coarse.transpose(2, 0, 1)

    sent = jnp.stack([along_z, got[:, 1], coarse], axis=1).reshape(wide, zw, 3, xc, yc)
    sent = sent.transpose(0, 3, 2, 1, 4).reshape(wide, 1, -1)
    got = lax.all_to_all(sent, "wide", split_axis=0, concat_axis=0, tiled=True)
    got = got.reshape(x_all, 3, zw * yc)

    along_x = jnp.dot(band(x_all), got[:, 0], precision=HIGHEST)
    z_pos = lax.axis_index("wide") * zw + lax.iota(jnp.int32, zw)
    y_pos = lax.axis_index("narrow") * yc + lax.iota(jnp.int32, yc)
    cover_zy = (cover(z_pos, z_all)[:, None] * cover(y_pos, y_all)[None, :]).reshape(-1)
    normalizer = cover(lax.iota(jnp.int32, x_all), x_all)[:, None] * cover_zy[None, :]
    filtered = along_x / normalizer
    inner = jnp.tanh(BETA * (filtered - ETA))
    slope = BETA * (1.0 - inner * inner) / SPAN_TANH
    density = (LOWER_TANH + inner) / SPAN_TANH
    weighted = slope * got[:, 2] * got[:, 1] / normalizer
    weighted = jnp.dot(band(x_all), weighted, precision=HIGHEST)

    sent = jnp.stack([density, weighted], axis=1).reshape(wide, 1, -1)
    got = lax.all_to_all(sent, "wide", split_axis=0, concat_axis=0, tiled=True)
    got = got.reshape(wide, xc, 2, zw, yc).transpose(0, 3, 2, 1, 4).reshape(z_all, 2, xc, yc)
    along_z = jnp.einsum("kz,zxy->kxy", band(z_all), got[:, 1], precision=HIGHEST)
    sent = jnp.stack([got[:, 0], along_z], axis=1).reshape(narrow, 1, -1)
    got = lax.all_to_all(sent, "narrow", split_axis=0, concat_axis=0, tiled=True)
    got = got.reshape(narrow, zc, 2, xc, yc).transpose(2, 1, 3, 0, 4).reshape(2, zc, xc, y_all)
    projected = got[0] * live + is_solid * (1.0 - is_void)
    design_sens = jnp.einsum("zxj,ij->zxi", got[1], band(y_all), precision=HIGHEST) * live
    return (projected, design_sens)


def solution(mesh):
    fields = P("wide", "narrow", None)
    cells = P("narrow", "wide", None)
    return jax.shard_map(
        per_device,
        mesh=mesh,
        in_specs=(fields, fields, fields, cells, cells, cells),
        out_specs=(cells, cells),
        check_vma=False,
    )
```

```python
import math

import jax
import jax.numpy as jnp
from jax import lax
from jax.experimental import pallas as pl
from jax.experimental.pallas import tpu as pltpu
from jax.sharding import PartitionSpec as P

RADIUS = 12
BETA = 32.0
ETA = 0.5
LOWER_TANH = math.tanh(BETA * ETA)
SPAN_TANH = math.tanh(BETA * ETA) + math.tanh(BETA * (1.0 - ETA))
F32, BF16 = jnp.float32, jnp.bfloat16
LANES = 128
XC, ZC, YC, ZW = 2, 16, 16, 4


def iota(shape, dim):
    return lax.broadcasted_iota(jnp.int32, shape, dim)


def tri(distance):
    return jnp.maximum(RADIUS + 1 - jnp.abs(distance), 0).astype(F32).astype(BF16)


def pieces(values):
    high = values.astype(BF16)
    rest = values - high.astype(F32)
    middle = rest.astype(BF16)
    return high, middle, (rest - middle.astype(F32)).astype(BF16)


def left_mul(weights, values):
    return sum(jnp.dot(weights, p, preferred_element_type=F32) for p in pieces(values))


def right_mul(values, weights):
    return sum(jnp.dot(p, weights, preferred_element_type=F32) for p in pieces(values))


def right_mul_t(weights, values):
    dims = (((1,), (1,)), ((), ()))
    return sum(lax.dot_general(weights, p, dims, preferred_element_type=F32) for p in pieces(values))


def roll_lanes(values, shift):
    shift %= values.shape[1]
    return pltpu.roll(values, shift, 1) if shift else values


def block_transpose(tile):
    block = iota((8, LANES), 1) // YC
    rolled = [roll_lanes(tile, YC * s) for s in range(8)]
    result = []
    for j in range(8):
        made = rolled[-j % 8][:8]
        for i in range(1, 8):
            made = jnp.where(block == i, rolled[(i - j) % 8][8 * i : 8 * i + 8], made)
        result.append(made)
    return result


def band_right(extent):
    return tri(iota((extent, extent), 0) - iota((extent, extent), 1))


def filter_y_kernel(design, solid, void, out):
    y_all = design.shape[2]
    cells = jnp.concatenate([design[:, x, :] for x in range(XC)], axis=0)
    along_y = right_mul(cells, band_right(y_all))
    live = jnp.concatenate(
        [(1.0 - solid[:, x, :].astype(F32)) * (1.0 - void[:, x, :].astype(F32)) for x in range(XC)], axis=0
    )
    both = jnp.concatenate([along_y, live], axis=0)
    for t in range(y_all // LANES):
        for m, tile in enumerate(block_transpose(both[:, LANES * t : LANES * (t + 1)])):
            out[64 * t + 8 * m : 64 * t + 8 * m + 8, :] = tile


def restrict_kernel(kirchhoff, adjoint, slope, x_before, x_after, y_before, y_after, out):
    x_fine, y_fine, z_fine = kirchhoff.shape
    row = iota((y_fine, z_fine), 0)
    lane = iota((y_fine, z_fine), 1)

    def diffs(f, field, x):
        centre = field[x]
        before = x_before[f, 0] if x == 0 else field[x - 1]
        after = x_after[f, 0] if x == x_fine - 1 else field[x + 1]
        grad_x = after - before
        up = jnp.where(row == 0, y_before[f, x], pltpu.roll(centre, 1, 0))
        down = jnp.where(row == y_fine - 1, y_after[f, x], pltpu.roll(centre, y_fine - 1, 0))
        left = jnp.where(lane == 0, 0.0, pltpu.roll(centre, 1, 1))
        right = jnp.where(lane == z_fine - 1, 0.0, pltpu.roll(centre, z_fine - 1, 1))
        return grad_x, down - up, right - left

    sensed = []
    for x in range(x_fine):
        k, a = diffs(0, kirchhoff, x), diffs(1, adjoint, x)
        product = k[0] * a[0] + k[1] * a[1] + k[2] * a[2]
        sensed.append(-0.25 * slope[x].astype(F32) * product)
    pairs = jnp.concatenate([sensed[2 * x] + sensed[2 * x + 1] for x in range(XC)], axis=0)
    rows_in, rows_out = XC * y_fine, XC * YC
    fold = (iota((rows_out, rows_in), 1) // 2 == iota((rows_out, rows_in), 0)).astype(F32).astype(BF16)
    pairs = left_mul(fold, pairs)
    z_quarter = iota((YC, z_fine), 1) // 2 % ZW
    spread = jnp.concatenate(
        [jnp.where(z_quarter == q, pairs[YC * x : YC * x + YC], 0.0) for x in range(XC) for q in range(ZW)], axis=0
    )
    wide = out.shape[0]
    gather = (iota((wide, z_fine), 1) // (2 * ZW) == iota((wide, z_fine), 0)).astype(F32).astype(BF16)
    out[...] = right_mul_t(gather, spread)


def filter_z_kernel(got, coarse, out, held, slots):
    rows = got.shape[0]
    narrow = rows // 8
    grid = got[...]
    lane = iota((rows, LANES), 1)
    half = lane // YC % 2
    after = jnp.where(half == 0, roll_lanes(grid, -YC), 0.0)
    before = jnp.where(half == 1, roll_lanes(grid, YC), 0.0)

    def base(dim):
        position = iota((rows, rows), dim)
        return ZC * (position // 8) + position % 8

    step = base(0) - base(1)
    weights = jnp.concatenate([tri(step), tri(step - 8), tri(step + 8)], axis=1)
    along_z = left_mul(weights, jnp.concatenate([grid, after, before], axis=0))
    held[...] = jnp.where(lane < LANES // 2, along_z, grid)
    block = iota((narrow, LANES), 1) // YC
    for low in range(2):
        picked = [held[pl.ds(4 * low + q, narrow, 8), :] for q in range(ZW)]
        for high in range(2):
            for a in range(2):
                made = None
                for x in range(XC):
                    for q in range(ZW):
                        target, source = ZW * x + q, 4 * a + 2 * x + high
                        moved = roll_lanes(picked[q], YC * (target - source))
                        made = moved if made is None else jnp.where(block == target, moved, made)
                slots.at[a][pl.ds(2 * high + low, narrow, 4), :] = made
    for a in range(2):
        out[:, LANES * a : LANES * (a + 1)] = slots[a]
    out[:, 2 * LANES :] = coarse[...]


def cover(positions, extent):
    low = jnp.maximum(RADIUS - positions, 0)
    high = jnp.maximum(RADIUS - (extent - 1 - positions), 0)
    return ((RADIUS + 1) ** 2 - low * (low + 1) // 2 - high * (high + 1) // 2).astype(F32)


def weigh_kernel(z_all, y_all, place, got, out):
    wide = got.shape[0]
    lane, row = iota((wide, LANES), 1), iota((wide, LANES), 0)
    step = 2 * (iota((wide, wide), 0) - iota((wide, wide), 1))
    weights = jnp.concatenate([tri(step), tri(step - 1), tri(step + 1)], axis=1)
    first = lane < LANES // 2

    def along_x(values):
        swapped = roll_lanes(values, LANES // 2)
        three = [values, jnp.where(first, swapped, 0.0), jnp.where(first, 0.0, swapped)]
        return left_mul(weights, jnp.concatenate(three, axis=0))

    cover_x = cover(XC * row + lane // (ZW * YC), XC * wide)
    cover_z = cover(place[0] * ZW + lane // YC % ZW, z_all)
    cover_y = cover(place[1] * YC + lane % YC, y_all)
    normalizer = cover_z * cover_x * cover_y
    filtered = along_x(got[:, :LANES]) / normalizer
    inner = jnp.tanh(BETA * (filtered - ETA))
    out[:, :LANES] = (LOWER_TANH + inner) / SPAN_TANH
    slope = BETA * (1.0 - inner * inner) / SPAN_TANH
    weighted = slope * got[:, 2 * LANES :] * got[:, LANES : 2 * LANES] / normalizer
    out[:, LANES:] = along_x(weighted)


def filter_z_back_kernel(got, out):
    wide = got.shape[0]
    density, weighted = got[:, :LANES], got[:, LANES:]
    quarter = iota((wide, LANES), 1) // YC % ZW
    step = ZW * (iota((wide, wide), 1) - iota((wide, wide), 0))
    weights, moved = [], []
    for d in range(1 - ZW, ZW):
        weights.append(tri(step + d))
        inside = (quarter + d >= 0) & (quarter + d < ZW)
        moved.append(jnp.where(inside, roll_lanes(weighted, -YC * d), 0.0))
    along_z = left_mul(jnp.concatenate(weights, axis=1), jnp.concatenate(moved, axis=0))
    per = ZC // ZW
    for n in range(wide // per):
        out[8 * n : 8 * n + per, :] = density[per * n : per * (n + 1)]
        out[8 * n + per : 8 * n + 2 * per, :] = along_z[per * n : per * (n + 1)]


def filter_y_back_kernel(got, solid, void, projected, sens, held):
    y_all = projected.shape[2]
    tiles = [block_transpose(got[64 * t : 64 * (t + 1), :]) for t in range(y_all // LANES)]
    lines = jnp.concatenate([jnp.concatenate(column, axis=0) for column in tiles], axis=1)
    along_y = right_mul(lines, band_right(y_all))
    per = ZC // ZW
    for x in range(XC):
        for q in range(ZW):
            at = 8 * (ZW * x + q)
            for t in range(y_all // LANES):
                lanes = slice(LANES * t, LANES * (t + 1))
                held[0, x, t, pl.ds(q, per, ZW), :] = lines[at : at + per, lanes]
                held[1, x, t, pl.ds(q, per, ZW), :] = along_y[at + per : at + 2 * per, lanes]
    for x in range(XC):
        is_solid, is_void = solid[:, x, :].astype(F32), void[:, x, :].astype(F32)
        live = (1.0 - is_solid) * (1.0 - is_void)
        density = jnp.concatenate([held[0, x, t] for t in range(y_all // LANES)], axis=1)
        smoothed = jnp.concatenate([held[1, x, t] for t in range(y_all // LANES)], axis=1)
        projected[:, x, :] = density * live + is_solid * (1.0 - is_void)
        sens[:, x, :] = smoothed * live


def call(kernel, shape, scratch=(), smem=()):
    def run(*args):
        specs = [pl.BlockSpec(memory_space=pltpu.SMEM if i in smem else pltpu.VMEM) for i in range(len(args))]
        out_shape = jax.tree.map(lambda s: jax.ShapeDtypeStruct(s, F32), shape, is_leaf=lambda s: isinstance(s[0], int))
        return pl.pallas_call(
            kernel,
            out_shape=out_shape,
            in_specs=specs,
            out_specs=jax.tree.map(lambda _: pl.BlockSpec(memory_space=pltpu.VMEM), out_shape),
            scratch_shapes=[pltpu.VMEM(s, F32) for s in scratch],
            compiler_params=pltpu.CompilerParams(vmem_limit_bytes=32 << 20),
        )(*args)

    return run


def neighbours(shards, axis, dim):
    count, length = lax.axis_size(axis), shards[0].shape[dim]
    up = [(i, i + 1) for i in range(count - 1)]
    down = [(j, i) for i, j in up]
    last = jnp.stack([lax.slice_in_dim(s, length - 1, length, axis=dim) for s in shards])
    initial = jnp.stack([lax.slice_in_dim(s, 0, 1, axis=dim) for s in shards])
    return lax.ppermute(last, axis, up), lax.ppermute(initial, axis, down)


def exchange(values, axis):
    return lax.all_to_all(values, axis, split_axis=0, concat_axis=0, tiled=True)


def exchange_rows(values, axis):
    rows, lanes = values.shape
    return exchange(values.reshape(rows, 1, lanes), axis).reshape(rows, lanes)


def per_device(kirchhoff, adjoint, penalty_slope, design, solid_mask, void_mask):
    wide, narrow = lax.axis_size("wide"), lax.axis_size("narrow")
    z_all, y_all = ZC * narrow, design.shape[2]

    sent = call(filter_y_kernel, (8 * narrow, LANES))(design, solid_mask, void_mask)
    got = exchange(sent, "narrow")

    y_before, y_after = neighbours((kirchhoff, adjoint), "narrow", 1)
    x_before, x_after = neighbours((kirchhoff, adjoint), "wide", 0)
    coarse = call(restrict_kernel, (wide, LANES))(
        kirchhoff, adjoint, penalty_slope, x_before, x_after, y_before, y_after
    )

    sent = call(filter_z_kernel, (wide, 3 * LANES), [(8 * narrow, LANES), (2, wide, LANES)])(got, coarse)
    place = jnp.stack([lax.axis_index("wide"), lax.axis_index("narrow")]).astype(jnp.int32)
    place, sent = lax.optimization_barrier((place, sent))
    got = exchange_rows(sent, "wide")

    def weigh(*refs):
        weigh_kernel(z_all, y_all, *refs)

    sent = call(weigh, (wide, 2 * LANES), smem=(0,))(place, got)
    got = exchange_rows(sent, "wide")
    sent = call(filter_z_back_kernel, (8 * narrow, LANES))(got)
    got = exchange(sent, "narrow")
    held = (2, XC, y_all // LANES, ZC, LANES)
    return call(filter_y_back_kernel, (design.shape, design.shape), [held])(got, solid_mask, void_mask)


def solution(mesh):
    fields = P("wide", "narrow", None)
    cells = P("narrow", "wide", None)
    return jax.shard_map(
        per_device,
        mesh=mesh,
        in_specs=(fields, fields, fields, cells, cells, cells),
        out_specs=(cells, cells),
        check_vma=False,
    )
```

```python
import math

import jax
import jax.numpy as jnp
from jax import lax
from jax.experimental import pallas as pl
from jax.experimental.pallas import tpu as pltpu
from jax.sharding import PartitionSpec as P

RADIUS = 12
BETA = 32.0
ETA = 0.5
LOWER_TANH = math.tanh(BETA * ETA)
SPAN_TANH = math.tanh(BETA * ETA) + math.tanh(BETA * (1.0 - ETA))
F32, BF16 = jnp.float32, jnp.bfloat16
LANES = 128
XC, ZC, YC, YW = 2, 16, 16, 4


def iota(shape, dim):
    return lax.broadcasted_iota(jnp.int32, shape, dim)


def tri(distance):
    return jnp.maximum(RADIUS + 1 - jnp.abs(distance), 0).astype(F32).astype(BF16)


def pieces(values):
    high = values.astype(BF16)
    rest = values - high.astype(F32)
    middle = rest.astype(BF16)
    return high, middle, (rest - middle.astype(F32)).astype(BF16)


def left_mul(weights, values):
    return sum(jnp.dot(weights, p, preferred_element_type=F32) for p in pieces(values))


def right_mul(values, weights):
    return sum(jnp.dot(p, weights, preferred_element_type=F32) for p in pieces(values))


def right_mul_t(weights, values):
    dims = (((1,), (1,)), ((), ()))
    return sum(lax.dot_general(weights, p, dims, preferred_element_type=F32) for p in pieces(values))


def roll_lanes(values, shift):
    shift %= values.shape[1]
    return pltpu.roll(values, shift, 1) if shift else values


def block_transpose(tile):
    r = tile.shape[0] // 8
    block = iota((r, LANES), 1) // ZC
    rolled = [roll_lanes(tile, ZC * s) for s in range(8)]
    result = []
    for j in range(8):
        made = rolled[-j % 8][:r]
        for i in range(1, 8):
            made = jnp.where(block == i, rolled[(i - j) % 8][r * i : r * (i + 1)], made)
        result.append(made)
    return result


def pack_kernel(kirchhoff, adjoint, design, y_last, y_first, x_last, x_first):
    x_fine, y_fine, _ = kirchhoff.shape
    y_all = design.shape[2]
    for out, y, x in ((y_last, y_fine - 1, x_fine - 1), (y_first, 0, 0)):
        for f, field in enumerate((kirchhoff, adjoint)):
            for k in range(x_fine):
                out[x_fine * f + k : x_fine * f + k + 1, :] = field[k, y : y + 1, :]
        for k in range(XC):
            out[2 * x_fine :, y_all * k : y_all * (k + 1)] = design[:, k, :]
    for out, x in ((x_last, x_fine - 1), (x_first, 0)):
        out[0] = kirchhoff[x]
        out[1] = adjoint[x]


def restrict_kernel(kirchhoff, adjoint, slope, x_before, x_after, n_before, n_after, out):
    x_fine, y_fine, z_fine = kirchhoff.shape
    row = iota((y_fine, z_fine), 0)
    lane = iota((y_fine, z_fine), 1)

    def diffs(f, field, x):
        centre = field[x]
        before = x_before[f] if x == 0 else field[x - 1]
        after = x_after[f] if x == x_fine - 1 else field[x + 1]
        grad_x = after - before
        at = x_fine * f + x
        up = jnp.where(row == 0, n_before[at : at + 1, :], pltpu.roll(centre, 1, 0))
        down = jnp.where(row == y_fine - 1, n_after[at : at + 1, :], pltpu.roll(centre, y_fine - 1, 0))
        left = jnp.where(lane == 0, 0.0, pltpu.roll(centre, 1, 1))
        right = jnp.where(lane == z_fine - 1, 0.0, pltpu.roll(centre, z_fine - 1, 1))
        return grad_x, down - up, right - left

    sensed = []
    for x in range(x_fine):
        k, a = diffs(0, kirchhoff, x), diffs(1, adjoint, x)
        product = k[0] * a[0] + k[1] * a[1] + k[2] * a[2]
        sensed.append(-0.25 * slope[x].astype(F32) * product)
    pairs = jnp.concatenate([sensed[2 * x] + sensed[2 * x + 1] for x in range(XC)], axis=0)
    shape = (XC * YC, XC * y_fine)
    made, given = iota(shape, 0), iota(shape, 1)
    y_made = YW * (made % YW) + made // YW % YW
    fold = (made // YC == given // y_fine) & (given % y_fine // 2 == y_made)
    pairs = left_mul(fold.astype(F32).astype(BF16), pairs)
    shape = (z_fine, z_fine // 2)
    pairs = right_mul(pairs, (iota(shape, 0) // 2 == iota(shape, 1)).astype(F32).astype(BF16))
    count = pairs.shape[1] // LANES
    parts = [pairs[YW * i : YW * (i + 1), LANES * t : LANES * (t + 1)] for i in range(8) for t in range(count)]
    for m, tile in enumerate(block_transpose(jnp.concatenate(parts, axis=0))):
        for t in range(count):
            at = YW * (8 * t + m)
            out[at : at + YW, :] = tile[YW * t : YW * (t + 1)]


def lines_of(values, wide):
    part = iota((wide, LANES), 1) // ZC % YW
    made = values[:wide]
    for r in range(1, YW):
        made = jnp.where(part == r, values[wide * r : wide * (r + 1)], made)
    return made


def design_kernel(design, solid, void, n_before, n_after, out):
    wide = out.shape[0]
    y_all = design.shape[2]
    skip = n_before.shape[0] - ZC
    shape = (ZC, 3 * ZC)
    weights = tri(iota(shape, 1) - iota(shape, 0) - ZC)
    along_z, live = [], []
    for x in range(XC):
        lanes = slice(y_all * x, y_all * (x + 1))
        planes = jnp.concatenate([n_before[skip:, lanes], design[:, x, :], n_after[skip:, lanes]], axis=0)
        along_z += [left_mul(weights, planes)] * YW
        is_live = (1.0 - solid[:, x, :].astype(F32)) * (1.0 - void[:, x, :].astype(F32))
        live += [is_live] * YW
    shape = (y_all, y_all)
    step = YW * (iota(shape, 0) % wide) + iota(shape, 0) // wide - iota(shape, 1)
    out[:, :LANES] = lines_of(right_mul_t(tri(step), jnp.concatenate(along_z, axis=0)), wide)
    place = (step == 0).astype(F32).astype(BF16)
    moved = lax.dot_general(
        place, jnp.concatenate(live, axis=0).astype(BF16), (((1,), (1,)), ((), ())), preferred_element_type=F32
    )
    out[:, LANES:] = lines_of(moved, wide)


def cover(positions, extent):
    low = jnp.maximum(RADIUS - positions, 0)
    high = jnp.maximum(RADIUS - (extent - 1 - positions), 0)
    return ((RADIUS + 1) ** 2 - low * (low + 1) // 2 - high * (high + 1) // 2).astype(F32)


def weigh_kernel(z_all, y_all, place, got, out):
    wide = got.shape[0]
    lane, row = iota((wide, LANES), 1), iota((wide, LANES), 0)
    step = 2 * (iota((wide, wide), 0) - iota((wide, wide), 1))
    weights = jnp.concatenate([tri(step), tri(step - 1), tri(step + 1)], axis=1)
    first = lane < LANES // 2

    def along_x(values):
        swapped = roll_lanes(values, LANES // 2)
        three = [values, jnp.where(first, swapped, 0.0), jnp.where(first, 0.0, swapped)]
        return left_mul(weights, jnp.concatenate(three, axis=0))

    cover_x = cover(XC * row + lane // (LANES // XC), XC * wide)
    cover_z = cover(place[1] * ZC + lane % ZC, z_all)
    cover_y = cover(place[0] * YW + lane // ZC % YW, y_all)
    normalizer = cover_z * cover_x * cover_y
    filtered = along_x(got[:, :LANES]) / normalizer
    inner = jnp.tanh(BETA * (filtered - ETA))
    out[:, :LANES] = (LOWER_TANH + inner) / SPAN_TANH
    slope = BETA * (1.0 - inner * inner) / SPAN_TANH
    weighted = slope * got[:, 2 * LANES :] * got[:, LANES : 2 * LANES] / normalizer
    out[:, LANES:] = along_x(weighted)


def along_lanes(values):
    turned = values.T
    rows = [[turned[ZC * (YW * x + r) : ZC * (YW * x + r + 1), :] for r in range(YW)] for x in range(XC)]
    return [jnp.concatenate(r, axis=1) for r in rows]


def y_steps(wide, y_all):
    shape = (YW * wide, y_all)
    return YW * (iota(shape, 0) % wide) + iota(shape, 0) // wide - iota(shape, 1)


def density_kernel(density, solid, void, projected):
    wide, y_all = density.shape[0], projected.shape[2]
    place = (y_steps(wide, y_all) == 0).astype(F32).astype(BF16)
    for x, lines in enumerate(along_lanes(density[...])):
        is_solid, is_void = solid[:, x, :].astype(F32), void[:, x, :].astype(F32)
        live = (1.0 - is_solid) * (1.0 - is_void)
        projected[:, x, :] = right_mul(lines, place) * live + is_solid * (1.0 - is_void)


def sens_kernel(before, own, after, solid, void, sens):
    wide, y_all = own.shape[0], sens.shape[2]
    given, made = iota((LANES, LANES), 0), iota((LANES, LANES), 1)
    step = jnp.where(given // ZC == made // ZC, given % ZC - made % ZC, 4 * ZC)
    weights = jnp.concatenate([tri(step - ZC), tri(step), tri(step + ZC)], axis=0)
    along_z = right_mul(jnp.concatenate([before[...], own[...], after[...]], axis=1), weights)
    weights = tri(y_steps(wide, y_all))
    for x, lines in enumerate(along_lanes(along_z)):
        live = (1.0 - solid[:, x, :].astype(F32)) * (1.0 - void[:, x, :].astype(F32))
        sens[:, x, :] = right_mul(lines, weights) * live


def call(kernel, shape, scratch=(), smem=()):
    def run(*args):
        specs = [pl.BlockSpec(memory_space=pltpu.SMEM if i in smem else pltpu.VMEM) for i in range(len(args))]
        out_shape = jax.tree.map(lambda s: jax.ShapeDtypeStruct(s, F32), shape, is_leaf=lambda s: isinstance(s[0], int))
        return pl.pallas_call(
            kernel,
            out_shape=out_shape,
            in_specs=specs,
            out_specs=jax.tree.map(lambda _: pl.BlockSpec(memory_space=pltpu.VMEM), out_shape),
            scratch_shapes=[pltpu.VMEM(s, F32) for s in scratch],
            compiler_params=pltpu.CompilerParams(vmem_limit_bytes=32 << 20),
        )(*args)

    return run


def to_sides(last, first, axis):
    up = [(i, i + 1) for i in range(lax.axis_size(axis) - 1)]
    return lax.ppermute(last, axis, up), lax.ppermute(first, axis, [(j, i) for i, j in up])


def exchange(values, axis):
    return lax.all_to_all(values, axis, split_axis=0, concat_axis=0, tiled=True)


def exchange_rows(values, axis):
    rows, lanes = values.shape
    return exchange(values.reshape(rows, 1, lanes), axis).reshape(rows, lanes)


def per_device(kirchhoff, adjoint, penalty_slope, design, solid_mask, void_mask):
    wide, narrow = lax.axis_size("wide"), lax.axis_size("narrow")
    z_all, y_all = ZC * narrow, design.shape[2]
    x_fine, y_fine, z_fine = kirchhoff.shape

    n_shape, x_shape = (2 * x_fine + ZC, z_fine), (2, y_fine, z_fine)
    packed = call(pack_kernel, (n_shape, n_shape, x_shape, x_shape))(kirchhoff, adjoint, design)
    n_before, n_after = to_sides(packed[0], packed[1], "narrow")
    x_before, x_after = to_sides(packed[2], packed[3], "wide")
    coarse = call(restrict_kernel, (YW * narrow, LANES))(
        kirchhoff, adjoint, penalty_slope, x_before, x_after, n_before, n_after
    )
    coarse = exchange(coarse, "narrow")
    lines = call(design_kernel, (wide, 2 * LANES))(design, solid_mask, void_mask, n_before, n_after)
    sent = jnp.concatenate([lines, coarse], axis=1)

    place = jnp.stack([lax.axis_index("wide"), lax.axis_index("narrow")]).astype(jnp.int32)
    place, sent = lax.optimization_barrier((place, sent))
    got = exchange_rows(sent, "wide")

    def weigh(*refs):
        weigh_kernel(z_all, y_all, *refs)

    sent = call(weigh, (wide, 2 * LANES), smem=(0,))(place, got)
    got = exchange_rows(sent, "wide")
    weighted = got[:, LANES:]
    before, after = to_sides(weighted, weighted, "narrow")
    projected = call(density_kernel, design.shape)(got[:, :LANES], solid_mask, void_mask)
    sens = call(sens_kernel, design.shape)(before, weighted, after, solid_mask, void_mask)
    return projected, sens


def solution(mesh):
    fields = P("wide", "narrow", None)
    cells = P("narrow", "wide", None)
    return jax.shard_map(
        per_device,
        mesh=mesh,
        in_specs=(fields, fields, fields, cells, cells, cells),
        out_specs=(cells, cells),
        check_vma=False,
    )
```

```python
import math

import jax
import jax.numpy as jnp
from jax import lax
from jax.experimental import pallas as pl
from jax.experimental.pallas import tpu as pltpu
from jax.sharding import PartitionSpec as P

RADIUS = 12
BETA = 32.0
ETA = 0.5
LOWER_TANH = math.tanh(BETA * ETA)
SPAN_TANH = math.tanh(BETA * ETA) + math.tanh(BETA * (1.0 - ETA))
F32, BF16 = jnp.float32, jnp.bfloat16
LANES = 128
XC, ZC, YC, YW = 2, 16, 16, 4


def iota(shape, dim):
    return lax.broadcasted_iota(jnp.int32, shape, dim)


def tri(distance):
    return jnp.maximum(RADIUS + 1 - jnp.abs(distance), 0).astype(F32).astype(BF16)


def pieces(values):
    high = values.astype(BF16)
    rest = values - high.astype(F32)
    middle = rest.astype(BF16)
    return high, middle, (rest - middle.astype(F32)).astype(BF16)


def left_mul(weights, values):
    return sum(jnp.dot(weights, p, preferred_element_type=F32) for p in pieces(values))


def right_mul(values, weights):
    return sum(jnp.dot(p, weights, preferred_element_type=F32) for p in pieces(values))


def right_mul_t(weights, values):
    dims = (((1,), (1,)), ((), ()))
    return sum(lax.dot_general(weights, p, dims, preferred_element_type=F32) for p in pieces(values))


def roll_lanes(values, shift):
    shift %= values.shape[1]
    return pltpu.roll(values, shift, 1) if shift else values


def block_transpose(tile):
    r = tile.shape[0] // 8
    block = iota((r, LANES), 1) // ZC
    rolled = [roll_lanes(tile, ZC * s) for s in range(8)]
    result = []
    for j in range(8):
        made = rolled[-j % 8][:r]
        for i in range(1, 8):
            made = jnp.where(block == i, rolled[(i - j) % 8][r * i : r * (i + 1)], made)
        result.append(made)
    return result


def pack_kernel(kirchhoff, adjoint, design, y_last, y_first):
    x_fine, y_fine, _ = kirchhoff.shape
    y_all = design.shape[2]
    for out, y, z in ((y_last, y_fine - 1, ZC - RADIUS), (y_first, 0, 0)):
        for f, field in enumerate((kirchhoff, adjoint)):
            for k in range(x_fine):
                for h in range(2):
                    at = 2 * (x_fine * f + k) + h
                    out[at : at + 1, :] = field[k, y : y + 1, y_all * h : y_all * (h + 1)]
        for k in range(XC):
            at = 4 * x_fine + RADIUS * k
            out[at : at + RADIUS, :] = design[:, k, :][z : z + RADIUS]


def restrict_kernel(kirchhoff, adjoint, slope, x_before, x_after, n_before, n_after, out):
    x_fine, y_fine, z_fine = kirchhoff.shape
    row = iota((y_fine, z_fine), 0)
    lane = iota((y_fine, z_fine), 1)

    def diffs(f, field, x):
        centre = field[x]
        before = x_before[f] if x == 0 else field[x - 1]
        after = x_after[f] if x == x_fine - 1 else field[x + 1]
        grad_x = after - before
        at = 2 * (x_fine * f + x)
        y_before, y_after = (jnp.concatenate([n[at : at + 1], n[at + 1 : at + 2]], axis=1) for n in (n_before, n_after))
        up = jnp.where(row == 0, y_before, pltpu.roll(centre, 1, 0))
        down = jnp.where(row == y_fine - 1, y_after, pltpu.roll(centre, y_fine - 1, 0))
        left = jnp.where(lane == 0, 0.0, pltpu.roll(centre, 1, 1))
        right = jnp.where(lane == z_fine - 1, 0.0, pltpu.roll(centre, z_fine - 1, 1))
        return grad_x, down - up, right - left

    sensed = []
    for x in range(x_fine):
        k, a = diffs(0, kirchhoff, x), diffs(1, adjoint, x)
        product = k[0] * a[0] + k[1] * a[1] + k[2] * a[2]
        sensed.append(-0.25 * slope[x].astype(F32) * product)
    pairs = jnp.concatenate([sensed[2 * x] + sensed[2 * x + 1] for x in range(XC)], axis=0)
    shape = (XC * YC, XC * y_fine)
    made, given = iota(shape, 0), iota(shape, 1)
    y_made = YW * (made % YW) + made // YW % YW
    fold = (made // YC == given // y_fine) & (given % y_fine // 2 == y_made)
    pairs = left_mul(fold.astype(F32).astype(BF16), pairs)
    shape = (z_fine, z_fine // 2)
    pairs = right_mul(pairs, (iota(shape, 0) // 2 == iota(shape, 1)).astype(F32).astype(BF16))
    count = pairs.shape[1] // LANES
    parts = [pairs[YW * i : YW * (i + 1), LANES * t : LANES * (t + 1)] for i in range(8) for t in range(count)]
    for m, tile in enumerate(block_transpose(jnp.concatenate(parts, axis=0))):
        for t in range(count):
            at = YW * (8 * t + m)
            out[at : at + YW, :] = tile[YW * t : YW * (t + 1)]


def lines_of(values, wide):
    part = iota((wide, LANES), 1) // ZC % YW
    made = values[:wide]
    for r in range(1, YW):
        made = jnp.where(part == r, values[wide * r : wide * (r + 1)], made)
    return made


def design_kernel(design, solid, void, n_before, n_after, out):
    wide = out.shape[0]
    y_all = design.shape[2]
    skip = n_before.shape[0] - XC * RADIUS
    shape = (ZC, ZC + 2 * RADIUS)
    weights = tri(iota(shape, 1) - iota(shape, 0) - RADIUS)
    along_z, live = [], []
    for x in range(XC):
        rows = slice(skip + RADIUS * x, skip + RADIUS * (x + 1))
        planes = jnp.concatenate([n_before[rows, :], design[:, x, :], n_after[rows, :]], axis=0)
        along_z += [left_mul(weights, planes)] * YW
        is_live = (1.0 - solid[:, x, :].astype(F32)) * (1.0 - void[:, x, :].astype(F32))
        live += [is_live] * YW
    shape = (y_all, y_all)
    step = YW * (iota(shape, 0) % wide) + iota(shape, 0) // wide - iota(shape, 1)
    out[:, :LANES] = lines_of(right_mul_t(tri(step), jnp.concatenate(along_z, axis=0)), wide)
    place = (step == 0).astype(F32).astype(BF16)
    moved = lax.dot_general(
        place, jnp.concatenate(live, axis=0).astype(BF16), (((1,), (1,)), ((), ())), preferred_element_type=F32
    )
    out[:, LANES:] = lines_of(moved, wide)


def cover(positions, extent):
    low = jnp.maximum(RADIUS - positions, 0)
    high = jnp.maximum(RADIUS - (extent - 1 - positions), 0)
    return ((RADIUS + 1) ** 2 - low * (low + 1) // 2 - high * (high + 1) // 2).astype(F32)


def weigh_kernel(z_all, y_all, place, got, out):
    wide = got.shape[0]
    lane, row = iota((wide, LANES), 1), iota((wide, LANES), 0)
    step = 2 * (iota((wide, wide), 0) - iota((wide, wide), 1))
    weights = jnp.concatenate([tri(step), tri(step - 1), tri(step + 1)], axis=1)
    first = lane < LANES // 2

    def along_x(values):
        swapped = roll_lanes(values, LANES // 2)
        three = [values, jnp.where(first, swapped, 0.0), jnp.where(first, 0.0, swapped)]
        return left_mul(weights, jnp.concatenate(three, axis=0))

    cover_x = cover(XC * row + lane // (LANES // XC), XC * wide)
    cover_z = cover(place[1] * ZC + lane % ZC, z_all)
    cover_y = cover(place[0] * YW + lane // ZC % YW, y_all)
    normalizer = cover_z * cover_x * cover_y
    filtered = along_x(got[:, :LANES]) / normalizer
    inner = jnp.tanh(BETA * (filtered - ETA))
    out[:, :LANES] = (LOWER_TANH + inner) / SPAN_TANH
    slope = BETA * (1.0 - inner * inner) / SPAN_TANH
    weighted = slope * got[:, 2 * LANES :] * got[:, LANES : 2 * LANES] / normalizer
    out[:, LANES:] = along_x(weighted)


def along_lanes(values):
    turned = values.T
    rows = [[turned[ZC * (YW * x + r) : ZC * (YW * x + r + 1), :] for r in range(YW)] for x in range(XC)]
    return [jnp.concatenate(r, axis=1) for r in rows]


def y_steps(wide, y_all):
    shape = (YW * wide, y_all)
    return YW * (iota(shape, 0) % wide) + iota(shape, 0) // wide - iota(shape, 1)


def pack_planes_kernel(got, last, first):
    rows = got.shape[0] // 4
    z = iota((rows, LANES), 1) % ZC
    skip = ZC - RADIUS
    values = got[:, LANES:]
    spare = values[3 * rows :]
    for g in range(3):
        own, at = values[rows * g : rows * (g + 1)], slice(rows * g, rows * (g + 1))
        last[at, :] = jnp.where(z >= skip, own, roll_lanes(spare, -skip * (g + 1)))
        first[at, :] = jnp.where(z < RADIUS, own, roll_lanes(spare, RADIUS - skip * g))


def unpack_planes(packed, is_last):
    rows = packed.shape[0] // 3
    z = iota((rows, LANES), 1) % ZC
    skip = ZC - RADIUS
    values = packed[...]
    spare = None
    for g in range(3):
        shift, start = (skip * (g + 1), skip * (g + 1)) if is_last else (skip * g - RADIUS, skip * g)
        moved = roll_lanes(values[rows * g : rows * (g + 1)], shift)
        spare = moved if spare is None else jnp.where((z >= start) & (z < start + skip), moved, spare)
    return jnp.concatenate([values, spare], axis=0)


def density_kernel(got, solid, void, projected):
    wide, y_all = got.shape[0], projected.shape[2]
    place = (y_steps(wide, y_all) == 0).astype(F32).astype(BF16)
    for x, lines in enumerate(along_lanes(got[:, :LANES])):
        is_solid, is_void = solid[:, x, :].astype(F32), void[:, x, :].astype(F32)
        live = (1.0 - is_solid) * (1.0 - is_void)
        projected[:, x, :] = right_mul(lines, place) * live + is_solid * (1.0 - is_void)


def sens_kernel(before, got, after, solid, void, sens):
    wide, y_all = got.shape[0], sens.shape[2]
    given, made = iota((LANES, LANES), 0), iota((LANES, LANES), 1)
    step = jnp.where(given // ZC == made // ZC, given % ZC - made % ZC, 4 * ZC)
    weights = jnp.concatenate([tri(step - ZC), tri(step), tri(step + ZC)], axis=0)
    three = [unpack_planes(before, True), got[:, LANES:], unpack_planes(after, False)]
    along_z = right_mul(jnp.concatenate(three, axis=1), weights)
    weights = tri(y_steps(wide, y_all))
    for x, lines in enumerate(along_lanes(along_z)):
        live = (1.0 - solid[:, x, :].astype(F32)) * (1.0 - void[:, x, :].astype(F32))
        sens[:, x, :] = right_mul(lines, weights) * live


def call(kernel, shape, scratch=(), smem=()):
    def run(*args):
        specs = [pl.BlockSpec(memory_space=pltpu.SMEM if i in smem else pltpu.VMEM) for i in range(len(args))]
        out_shape = jax.tree.map(lambda s: jax.ShapeDtypeStruct(s, F32), shape, is_leaf=lambda s: isinstance(s[0], int))
        return pl.pallas_call(
            kernel,
            out_shape=out_shape,
            in_specs=specs,
            out_specs=jax.tree.map(lambda _: pl.BlockSpec(memory_space=pltpu.VMEM), out_shape),
            scratch_shapes=[pltpu.VMEM(s, F32) for s in scratch],
            compiler_params=pltpu.CompilerParams(vmem_limit_bytes=32 << 20),
        )(*args)

    return run


def to_sides(last, first, axis):
    up = [(i, i + 1) for i in range(lax.axis_size(axis) - 1)]
    return lax.ppermute(last, axis, up), lax.ppermute(first, axis, [(j, i) for i, j in up])


def exchange(values, axis):
    return lax.all_to_all(values, axis, split_axis=0, concat_axis=0, tiled=True)


def exchange_rows(values, axis):
    rows, lanes = values.shape
    return exchange(values.reshape(rows, 1, lanes), axis).reshape(rows, lanes)


def per_device(kirchhoff, adjoint, penalty_slope, design, solid_mask, void_mask):
    wide, narrow = lax.axis_size("wide"), lax.axis_size("narrow")
    z_all, y_all = ZC * narrow, design.shape[2]
    x_fine = kirchhoff.shape[0]

    x_last, x_first = (jnp.stack([kirchhoff[x], adjoint[x]]) for x in (x_fine - 1, 0))
    x_before, x_after = to_sides(x_last, x_first, "wide")
    packed = (4 * x_fine + XC * RADIUS, y_all)
    n_before, n_after = to_sides(*call(pack_kernel, (packed, packed))(kirchhoff, adjoint, design), "narrow")
    coarse = call(restrict_kernel, (YW * narrow, LANES))(
        kirchhoff, adjoint, penalty_slope, x_before, x_after, n_before, n_after
    )
    lines = call(design_kernel, (wide, 2 * LANES))(design, solid_mask, void_mask, n_before, n_after)
    place = jnp.stack([lax.axis_index("wide"), lax.axis_index("narrow")]).astype(jnp.int32)
    lines, coarse, place = lax.optimization_barrier((lines, coarse, place))
    coarse = exchange(coarse, "narrow")
    sent = jnp.concatenate([lines, coarse], axis=1)

    got = exchange_rows(sent, "wide")

    def weigh(*refs):
        weigh_kernel(z_all, y_all, *refs)

    sent = call(weigh, (wide, 2 * LANES), smem=(0,))(place, got)
    got = exchange_rows(sent, "wide")
    packed = (3 * wide // 4, LANES)
    before, after = to_sides(*call(pack_planes_kernel, (packed, packed))(got), "narrow")
    projected = call(density_kernel, design.shape)(got, solid_mask, void_mask)
    sens = call(sens_kernel, design.shape)(before, got, after, solid_mask, void_mask)
    return projected, sens


def solution(mesh):
    fields = P("wide", "narrow", None)
    cells = P("narrow", "wide", None)
    return jax.shard_map(
        per_device,
        mesh=mesh,
        in_specs=(fields, fields, fields, cells, cells, cells),
        out_specs=(cells, cells),
        check_vma=False,
    )
```

```python
import math

import jax
import jax.numpy as jnp
from jax import lax
from jax.experimental import pallas as pl
from jax.experimental.pallas import tpu as pltpu
from jax.sharding import PartitionSpec as P

RADIUS = 12
BETA = 32.0
ETA = 0.5
LOWER_TANH = math.tanh(BETA * ETA)
SPAN_TANH = math.tanh(BETA * ETA) + math.tanh(BETA * (1.0 - ETA))
F32, BF16 = jnp.float32, jnp.bfloat16
LANES = 128
XC, ZC, YC, YW = 2, 16, 16, 4


def iota(shape, dim):
    return lax.broadcasted_iota(jnp.int32, shape, dim)


def tri(distance):
    return jnp.maximum(RADIUS + 1 - jnp.abs(distance), 0).astype(F32).astype(BF16)


def pieces(values):
    high = values.astype(BF16)
    rest = values - high.astype(F32)
    middle = rest.astype(BF16)
    return high, middle, (rest - middle.astype(F32)).astype(BF16)


def left_mul(weights, values):
    return sum(jnp.dot(weights, p, preferred_element_type=F32) for p in pieces(values))


def right_mul(values, weights):
    return sum(jnp.dot(p, weights, preferred_element_type=F32) for p in pieces(values))


def right_mul_t(weights, values):
    dims = (((1,), (1,)), ((), ()))
    return sum(lax.dot_general(weights, p, dims, preferred_element_type=F32) for p in pieces(values))


def roll_lanes(values, shift):
    shift %= values.shape[1]
    return pltpu.roll(values, shift, 1) if shift else values


def block_transpose(tile):
    r = tile.shape[0] // 8
    block = iota((r, LANES), 1) // ZC
    rolled = [roll_lanes(tile, ZC * s) for s in range(8)]
    result = []
    for j in range(8):
        made = rolled[-j % 8][:r]
        for i in range(1, 8):
            made = jnp.where(block == i, rolled[(i - j) % 8][r * i : r * (i + 1)], made)
        result.append(made)
    return result


def is_even(axis):
    return lax.rem(lax.axis_index(axis), 2) == 0


def by_side(even, of_first, of_second):
    return jnp.where(even, of_second, of_first), jnp.where(even, of_first, of_second)


def pack_kernel(kirchhoff, adjoint, design, to_first, to_second):
    even = is_even("narrow")
    x_fine, y_fine, _ = kirchhoff.shape
    y_all = design.shape[2]

    def put(rows, before, after):
        to_first[rows, :] = jnp.where(even, after, before)
        to_second[rows, :] = jnp.where(even, before, after)

    for f, field in enumerate((kirchhoff, adjoint)):
        for k in range(x_fine):
            for h in range(2):
                at, lanes = 2 * (x_fine * f + k) + h, slice(y_all * h, y_all * (h + 1))
                put(slice(at, at + 1), field[k, 0:1, lanes], field[k, y_fine - 1 : y_fine, lanes])
    for k in range(XC):
        at = 4 * x_fine + RADIUS * k
        planes = design[:, k, :]
        put(slice(at, at + RADIUS), planes[:RADIUS], planes[ZC - RADIUS :])


def restrict_kernel(kirchhoff, adjoint, slope, x_first, x_second, n_first, n_second, out):
    x_fine, y_fine, z_fine = kirchhoff.shape
    row = iota((y_fine, z_fine), 0)
    lane = iota((y_fine, z_fine), 1)
    x_even, n_even = is_even("wide"), is_even("narrow")

    def diffs(f, field, x):
        centre = field[x]
        x_before, x_after = by_side(x_even, x_first[f], x_second[f])
        before = x_before if x == 0 else field[x - 1]
        after = x_after if x == x_fine - 1 else field[x + 1]
        grad_x = after - before
        at = 2 * (x_fine * f + x)
        y_before, y_after = by_side(
            n_even, *(jnp.concatenate([n[at : at + 1], n[at + 1 : at + 2]], axis=1) for n in (n_first, n_second))
        )
        up = jnp.where(row == 0, y_before, pltpu.roll(centre, 1, 0))
        down = jnp.where(row == y_fine - 1, y_after, pltpu.roll(centre, y_fine - 1, 0))
        left = jnp.where(lane == 0, 0.0, pltpu.roll(centre, 1, 1))
        right = jnp.where(lane == z_fine - 1, 0.0, pltpu.roll(centre, z_fine - 1, 1))
        return grad_x, down - up, right - left

    sensed = []
    for x in range(x_fine):
        k, a = diffs(0, kirchhoff, x), diffs(1, adjoint, x)
        product = k[0] * a[0] + k[1] * a[1] + k[2] * a[2]
        sensed.append(-0.25 * slope[x].astype(F32) * product)
    pairs = jnp.concatenate([sensed[2 * x] + sensed[2 * x + 1] for x in range(XC)], axis=0)
    shape = (XC * YC, XC * y_fine)
    made, given = iota(shape, 0), iota(shape, 1)
    y_made = YW * (made % YW) + made // YW % YW
    fold = (made // YC == given // y_fine) & (given % y_fine // 2 == y_made)
    pairs = left_mul(fold.astype(F32).astype(BF16), pairs)
    shape = (z_fine, z_fine // 2)
    pairs = right_mul(pairs, (iota(shape, 0) // 2 == iota(shape, 1)).astype(F32).astype(BF16))
    count = pairs.shape[1] // LANES
    parts = [pairs[YW * i : YW * (i + 1), LANES * t : LANES * (t + 1)] for i in range(8) for t in range(count)]
    for m, tile in enumerate(block_transpose(jnp.concatenate(parts, axis=0))):
        for t in range(count):
            at = YW * (8 * t + m)
            out[at : at + YW, :] = tile[YW * t : YW * (t + 1)]


def lines_of(values, wide):
    part = iota((wide, LANES), 1) // ZC % YW
    made = values[:wide]
    for r in range(1, YW):
        made = jnp.where(part == r, values[wide * r : wide * (r + 1)], made)
    return made


def design_kernel(design, solid, void, n_first, n_second, out):
    wide = out.shape[0]
    y_all = design.shape[2]
    skip = n_first.shape[0] - XC * RADIUS
    shape = (ZC, ZC + 2 * RADIUS)
    weights = tri(iota(shape, 1) - iota(shape, 0) - RADIUS)
    along_z, live = [], []
    for x in range(XC):
        rows = slice(skip + RADIUS * x, skip + RADIUS * (x + 1))
        before, after = by_side(is_even("narrow"), n_first[rows, :], n_second[rows, :])
        planes = jnp.concatenate([before, design[:, x, :], after], axis=0)
        along_z += [left_mul(weights, planes)] * YW
        is_live = (1.0 - solid[:, x, :].astype(F32)) * (1.0 - void[:, x, :].astype(F32))
        live += [is_live] * YW
    shape = (y_all, y_all)
    step = YW * (iota(shape, 0) % wide) + iota(shape, 0) // wide - iota(shape, 1)
    out[:, :LANES] = lines_of(right_mul_t(tri(step), jnp.concatenate(along_z, axis=0)), wide)
    place = (step == 0).astype(F32).astype(BF16)
    moved = lax.dot_general(
        place, jnp.concatenate(live, axis=0).astype(BF16), (((1,), (1,)), ((), ())), preferred_element_type=F32
    )
    out[:, LANES:] = lines_of(moved, wide)


def cover(positions, extent):
    low = jnp.maximum(RADIUS - positions, 0)
    high = jnp.maximum(RADIUS - (extent - 1 - positions), 0)
    return ((RADIUS + 1) ** 2 - low * (low + 1) // 2 - high * (high + 1) // 2).astype(F32)


def weigh_kernel(z_all, y_all, place, got, out):
    wide = got.shape[0]
    lane, row = iota((wide, LANES), 1), iota((wide, LANES), 0)
    step = 2 * (iota((wide, wide), 0) - iota((wide, wide), 1))
    weights = jnp.concatenate([tri(step), tri(step - 1), tri(step + 1)], axis=1)
    first = lane < LANES // 2

    def along_x(values):
        swapped = roll_lanes(values, LANES // 2)
        three = [values, jnp.where(first, swapped, 0.0), jnp.where(first, 0.0, swapped)]
        return left_mul(weights, jnp.concatenate(three, axis=0))

    cover_x = cover(XC * row + lane // (LANES // XC), XC * wide)
    cover_z = cover(place[1] * ZC + lane % ZC, z_all)
    cover_y = cover(place[0] * YW + lane // ZC % YW, y_all)
    normalizer = cover_z * cover_x * cover_y
    filtered = along_x(got[:, :LANES]) / normalizer
    inner = jnp.tanh(BETA * (filtered - ETA))
    out[:, :LANES] = (LOWER_TANH + inner) / SPAN_TANH
    slope = BETA * (1.0 - inner * inner) / SPAN_TANH
    weighted = slope * got[:, 2 * LANES :] * got[:, LANES : 2 * LANES] / normalizer
    out[:, LANES:] = along_x(weighted)


def along_lanes(values):
    turned = values.T
    rows = [[turned[ZC * (YW * x + r) : ZC * (YW * x + r + 1), :] for r in range(YW)] for x in range(XC)]
    return [jnp.concatenate(r, axis=1) for r in rows]


def y_steps(wide, y_all):
    shape = (YW * wide, y_all)
    return YW * (iota(shape, 0) % wide) + iota(shape, 0) // wide - iota(shape, 1)


def pack_planes_kernel(got, to_first, to_second):
    rows = got.shape[0] // 4
    z = iota((rows, LANES), 1) % ZC
    skip = ZC - RADIUS
    even = is_even("narrow")
    values = got[:, LANES:]
    spare = values[3 * rows :]
    for g in range(3):
        own, at = values[rows * g : rows * (g + 1)], slice(rows * g, rows * (g + 1))
        after = jnp.where(z >= skip, own, roll_lanes(spare, -skip * (g + 1)))
        before = jnp.where(z < RADIUS, own, roll_lanes(spare, RADIUS - skip * g))
        to_first[at, :] = jnp.where(even, after, before)
        to_second[at, :] = jnp.where(even, before, after)


def unpack_planes(packed, is_last):
    rows = packed.shape[0] // 3
    z = iota((rows, LANES), 1) % ZC
    skip = ZC - RADIUS
    values = packed
    spare = None
    for g in range(3):
        shift, start = (skip * (g + 1), skip * (g + 1)) if is_last else (skip * g - RADIUS, skip * g)
        moved = roll_lanes(values[rows * g : rows * (g + 1)], shift)
        spare = moved if spare is None else jnp.where((z >= start) & (z < start + skip), moved, spare)
    return jnp.concatenate([values, spare], axis=0)


def density_kernel(got, solid, void, projected):
    wide, y_all = got.shape[0], projected.shape[2]
    place = (y_steps(wide, y_all) == 0).astype(F32).astype(BF16)
    for x, lines in enumerate(along_lanes(got[:, :LANES])):
        is_solid, is_void = solid[:, x, :].astype(F32), void[:, x, :].astype(F32)
        live = (1.0 - is_solid) * (1.0 - is_void)
        projected[:, x, :] = right_mul(lines, place) * live + is_solid * (1.0 - is_void)


def sens_kernel(first, got, second, solid, void, sens):
    before, after = by_side(is_even("narrow"), first[...], second[...])
    wide, y_all = got.shape[0], sens.shape[2]
    given, made = iota((LANES, LANES), 0), iota((LANES, LANES), 1)
    step = jnp.where(given // ZC == made // ZC, given % ZC - made % ZC, 4 * ZC)
    weights = jnp.concatenate([tri(step - ZC), tri(step), tri(step + ZC)], axis=0)
    three = [unpack_planes(before, True), got[:, LANES:], unpack_planes(after, False)]
    along_z = right_mul(jnp.concatenate(three, axis=1), weights)
    weights = tri(y_steps(wide, y_all))
    for x, lines in enumerate(along_lanes(along_z)):
        live = (1.0 - solid[:, x, :].astype(F32)) * (1.0 - void[:, x, :].astype(F32))
        sens[:, x, :] = right_mul(lines, weights) * live


def call(kernel, shape, scratch=(), smem=()):
    def run(*args):
        specs = [pl.BlockSpec(memory_space=pltpu.SMEM if i in smem else pltpu.VMEM) for i in range(len(args))]
        out_shape = jax.tree.map(lambda s: jax.ShapeDtypeStruct(s, F32), shape, is_leaf=lambda s: isinstance(s[0], int))
        return pl.pallas_call(
            kernel,
            out_shape=out_shape,
            in_specs=specs,
            out_specs=jax.tree.map(lambda _: pl.BlockSpec(memory_space=pltpu.VMEM), out_shape),
            scratch_shapes=[pltpu.VMEM(s, F32) for s in scratch],
            compiler_params=pltpu.CompilerParams(vmem_limit_bytes=32 << 20),
        )(*args)

    return run


def swap(to_first, to_second, axis):
    count = lax.axis_size(axis)
    pairs = [[(i, i + 1) for i in range(start, count - 1, 2)] for start in (0, 1)]
    both = [[*p, *((j, i) for i, j in p)] for p in pairs]
    return lax.ppermute(to_first, axis, both[0]), lax.ppermute(to_second, axis, both[1])


def exchange(values, axis):
    return lax.all_to_all(values, axis, split_axis=0, concat_axis=0, tiled=True)


def exchange_rows(values, axis):
    rows, lanes = values.shape
    return exchange(values.reshape(rows, 1, lanes), axis).reshape(rows, lanes)


def per_device(kirchhoff, adjoint, penalty_slope, design, solid_mask, void_mask):
    wide, narrow = lax.axis_size("wide"), lax.axis_size("narrow")
    z_all, y_all = ZC * narrow, design.shape[2]
    x_fine = kirchhoff.shape[0]

    sides = [jnp.stack([kirchhoff[x], adjoint[x]]) for x in (0, x_fine - 1)]
    even = is_even("wide")
    x_first, x_second = swap(jnp.where(even, sides[1], sides[0]), jnp.where(even, sides[0], sides[1]), "wide")
    packed = (4 * x_fine + XC * RADIUS, y_all)
    n_first, n_second = swap(*call(pack_kernel, (packed, packed))(kirchhoff, adjoint, design), "narrow")
    coarse = call(restrict_kernel, (YW * narrow, LANES))(
        kirchhoff, adjoint, penalty_slope, x_first, x_second, n_first, n_second
    )
    lines = call(design_kernel, (wide, 2 * LANES))(design, solid_mask, void_mask, n_first, n_second)
    place = jnp.stack([lax.axis_index("wide"), lax.axis_index("narrow")]).astype(jnp.int32)
    lines, coarse, place = lax.optimization_barrier((lines, coarse, place))
    coarse = exchange(coarse, "narrow")
    sent = jnp.concatenate([lines, coarse], axis=1)

    got = exchange_rows(sent, "wide")

    def weigh(*refs):
        weigh_kernel(z_all, y_all, *refs)

    sent = call(weigh, (wide, 2 * LANES), smem=(0,))(place, got)
    got = exchange_rows(sent, "wide")
    packed = (3 * wide // 4, LANES)
    first, second = swap(*call(pack_planes_kernel, (packed, packed))(got), "narrow")
    projected = call(density_kernel, design.shape)(got, solid_mask, void_mask)
    sens = call(sens_kernel, design.shape)(first, got, second, solid_mask, void_mask)
    return projected, sens


def solution(mesh):
    fields = P("wide", "narrow", None)
    cells = P("narrow", "wide", None)
    return jax.shard_map(
        per_device,
        mesh=mesh,
        in_specs=(fields, fields, fields, cells, cells, cells),
        out_specs=(cells, cells),
        check_vma=False,
    )
```

```python
import math

import jax
import jax.numpy as jnp
from jax import lax
from jax.experimental import pallas as pl
from jax.experimental.pallas import tpu as pltpu
from jax.sharding import PartitionSpec as P

RADIUS = 12
BETA = 32.0
ETA = 0.5
LOWER_TANH = math.tanh(BETA * ETA)
SPAN_TANH = math.tanh(BETA * ETA) + math.tanh(BETA * (1.0 - ETA))
F32, BF16 = jnp.float32, jnp.bfloat16
LANES = 128
XC, ZC, YC, YW = 2, 16, 16, 4


def iota(shape, dim):
    return lax.broadcasted_iota(jnp.int32, shape, dim)


def tri(distance):
    return jnp.maximum(RADIUS + 1 - jnp.abs(distance), 0).astype(F32).astype(BF16)


def pieces(values):
    high = values.astype(BF16)
    rest = values - high.astype(F32)
    middle = rest.astype(BF16)
    return high, middle, (rest - middle.astype(F32)).astype(BF16)


def left_mul(weights, values):
    return sum(jnp.dot(weights, p, preferred_element_type=F32) for p in pieces(values))


def right_mul(values, weights):
    return sum(jnp.dot(p, weights, preferred_element_type=F32) for p in pieces(values))


def right_mul_t(weights, values):
    dims = (((1,), (1,)), ((), ()))
    return sum(lax.dot_general(weights, p, dims, preferred_element_type=F32) for p in pieces(values))


def roll_lanes(values, shift):
    shift %= values.shape[1]
    return pltpu.roll(values, shift, 1) if shift else values


def block_transpose(tile):
    r = tile.shape[0] // 8
    block = iota((r, LANES), 1) // ZC
    rolled = [roll_lanes(tile, ZC * s) for s in range(8)]
    result = []
    for j in range(8):
        made = rolled[-j % 8][:r]
        for i in range(1, 8):
            made = jnp.where(block == i, rolled[(i - j) % 8][r * i : r * (i + 1)], made)
        result.append(made)
    return result


def is_even(axis):
    return lax.rem(lax.axis_index(axis), 2) == 0


def by_side(even, of_first, of_second):
    return jnp.where(even, of_second, of_first), jnp.where(even, of_first, of_second)


def pack_kernel(kirchhoff, adjoint, design, to_first, to_second):
    even = is_even("narrow")
    x_fine, y_fine, _ = kirchhoff.shape
    y_all = design.shape[2]

    def put(rows, before, after):
        to_first[rows, :] = jnp.where(even, after, before)
        to_second[rows, :] = jnp.where(even, before, after)

    for f, field in enumerate((kirchhoff, adjoint)):
        for k in range(x_fine):
            for h in range(2):
                at, lanes = 2 * (x_fine * f + k) + h, slice(y_all * h, y_all * (h + 1))
                put(slice(at, at + 1), field[k, 0:1, lanes], field[k, y_fine - 1 : y_fine, lanes])
    for k in range(XC):
        at = 4 * x_fine + RADIUS * k
        planes = design[:, k, :]
        put(slice(at, at + RADIUS), planes[:RADIUS], planes[ZC - RADIUS :])


def restrict_kernel(kirchhoff, adjoint, slope, x_first, x_second, n_first, n_second, out):
    x_fine, y_fine, z_fine = kirchhoff.shape
    row = iota((y_fine, z_fine), 0)
    lane = iota((y_fine, z_fine), 1)
    x_even, n_even = is_even("wide"), is_even("narrow")

    def diffs(f, field, x):
        centre = field[x]
        x_before, x_after = by_side(x_even, x_first[f], x_second[f])
        before = x_before if x == 0 else field[x - 1]
        after = x_after if x == x_fine - 1 else field[x + 1]
        grad_x = after - before
        at = 2 * (x_fine * f + x)
        y_before, y_after = by_side(
            n_even, *(jnp.concatenate([n[at : at + 1], n[at + 1 : at + 2]], axis=1) for n in (n_first, n_second))
        )
        up = jnp.where(row == 0, y_before, pltpu.roll(centre, 1, 0))
        down = jnp.where(row == y_fine - 1, y_after, pltpu.roll(centre, y_fine - 1, 0))
        left = jnp.where(lane == 0, 0.0, pltpu.roll(centre, 1, 1))
        right = jnp.where(lane == z_fine - 1, 0.0, pltpu.roll(centre, z_fine - 1, 1))
        return grad_x, down - up, right - left

    sensed = []
    for x in range(x_fine):
        k, a = diffs(0, kirchhoff, x), diffs(1, adjoint, x)
        product = k[0] * a[0] + k[1] * a[1] + k[2] * a[2]
        sensed.append(-0.25 * slope[x].astype(F32) * product)
    pairs = jnp.concatenate([sensed[2 * x] + sensed[2 * x + 1] for x in range(XC)], axis=0)
    shape = (XC * YC, XC * y_fine)
    made, given = iota(shape, 0), iota(shape, 1)
    y_made = YW * (made % YW) + made // YW % YW
    fold = (made // YC == given // y_fine) & (given % y_fine // 2 == y_made)
    pairs = left_mul(fold.astype(F32).astype(BF16), pairs)
    shape = (z_fine, z_fine // 2)
    pairs = right_mul(pairs, (iota(shape, 0) // 2 == iota(shape, 1)).astype(F32).astype(BF16))
    count = pairs.shape[1] // LANES
    parts = [pairs[YW * i : YW * (i + 1), LANES * t : LANES * (t + 1)] for i in range(8) for t in range(count)]
    for m, tile in enumerate(block_transpose(jnp.concatenate(parts, axis=0))):
        for t in range(count):
            at = YW * (8 * t + m)
            out[at : at + YW, :] = tile[YW * t : YW * (t + 1)]


def lines_of(values, wide):
    part = iota((wide, LANES), 1) // ZC % YW
    made = values[:wide]
    for r in range(1, YW):
        made = jnp.where(part == r, values[wide * r : wide * (r + 1)], made)
    return made


def design_kernel(design, solid, void, n_first, n_second, out):
    wide = out.shape[0]
    y_all = design.shape[2]
    skip = n_first.shape[0] - XC * RADIUS
    shape = (ZC, ZC + 2 * RADIUS)
    weights = tri(iota(shape, 1) - iota(shape, 0) - RADIUS)
    along_z, live = [], []
    for x in range(XC):
        rows = slice(skip + RADIUS * x, skip + RADIUS * (x + 1))
        before, after = by_side(is_even("narrow"), n_first[rows, :], n_second[rows, :])
        planes = jnp.concatenate([before, design[:, x, :], after], axis=0)
        along_z += [left_mul(weights, planes)] * YW
        is_live = (1.0 - solid[:, x, :].astype(F32)) * (1.0 - void[:, x, :].astype(F32))
        live += [is_live] * YW
    shape = (y_all, y_all)
    step = YW * (iota(shape, 0) % wide) + iota(shape, 0) // wide - iota(shape, 1)
    out[:, :LANES] = lines_of(right_mul_t(tri(step), jnp.concatenate(along_z, axis=0)), wide)
    place = (step == 0).astype(F32).astype(BF16)
    moved = lax.dot_general(
        place, jnp.concatenate(live, axis=0).astype(BF16), (((1,), (1,)), ((), ())), preferred_element_type=F32
    )
    out[:, LANES:] = lines_of(moved, wide)


def cover(positions, extent):
    low = jnp.maximum(RADIUS - positions, 0)
    high = jnp.maximum(RADIUS - (extent - 1 - positions), 0)
    return ((RADIUS + 1) ** 2 - low * (low + 1) // 2 - high * (high + 1) // 2).astype(F32)


def weigh_kernel(z_all, y_all, place, got, out):
    wide = got.shape[0]
    lane, row = iota((wide, LANES), 1), iota((wide, LANES), 0)
    step = 2 * (iota((wide, wide), 0) - iota((wide, wide), 1))
    weights = jnp.concatenate([tri(step), tri(step - 1), tri(step + 1)], axis=1)
    first = lane < LANES // 2

    def along_x(values):
        swapped = roll_lanes(values, LANES // 2)
        three = [values, jnp.where(first, swapped, 0.0), jnp.where(first, 0.0, swapped)]
        return left_mul(weights, jnp.concatenate(three, axis=0))

    cover_x = cover(XC * row + lane // (LANES // XC), XC * wide)
    cover_z = cover(place[1] * ZC + lane % ZC, z_all)
    cover_y = cover(place[0] * YW + lane // ZC % YW, y_all)
    normalizer = cover_z * cover_x * cover_y
    filtered = along_x(got[:, :LANES]) / normalizer
    inner = jnp.tanh(BETA * (filtered - ETA))
    out[:, :LANES] = (LOWER_TANH + inner) / SPAN_TANH
    slope = BETA * (1.0 - inner * inner) / SPAN_TANH
    weighted = slope * got[:, LANES:] / normalizer
    out[:, LANES:] = along_x(weighted)


def along_lanes(values):
    turned = values.T
    rows = [[turned[ZC * (YW * x + r) : ZC * (YW * x + r + 1), :] for r in range(YW)] for x in range(XC)]
    return [jnp.concatenate(r, axis=1) for r in rows]


def y_steps(wide, y_all):
    shape = (YW * wide, y_all)
    return YW * (iota(shape, 0) % wide) + iota(shape, 0) // wide - iota(shape, 1)


def pack_planes_kernel(got, to_first, to_second):
    rows = got.shape[0] // 4
    z = iota((rows, LANES), 1) % ZC
    skip = ZC - RADIUS
    even = is_even("narrow")
    values = got[:, LANES:]
    spare = values[3 * rows :]
    for g in range(3):
        own, at = values[rows * g : rows * (g + 1)], slice(rows * g, rows * (g + 1))
        after = jnp.where(z >= skip, own, roll_lanes(spare, -skip * (g + 1)))
        before = jnp.where(z < RADIUS, own, roll_lanes(spare, RADIUS - skip * g))
        to_first[at, :] = jnp.where(even, after, before)
        to_second[at, :] = jnp.where(even, before, after)


def unpack_planes(packed, is_last):
    rows = packed.shape[0] // 3
    z = iota((rows, LANES), 1) % ZC
    skip = ZC - RADIUS
    values = packed
    spare = None
    for g in range(3):
        shift, start = (skip * (g + 1), skip * (g + 1)) if is_last else (skip * g - RADIUS, skip * g)
        moved = roll_lanes(values[rows * g : rows * (g + 1)], shift)
        spare = moved if spare is None else jnp.where((z >= start) & (z < start + skip), moved, spare)
    return jnp.concatenate([values, spare], axis=0)


def density_kernel(got, solid, void, projected):
    wide, y_all = got.shape[0], projected.shape[2]
    place = (y_steps(wide, y_all) == 0).astype(F32).astype(BF16)
    for x, lines in enumerate(along_lanes(got[:, :LANES])):
        is_solid, is_void = solid[:, x, :].astype(F32), void[:, x, :].astype(F32)
        live = (1.0 - is_solid) * (1.0 - is_void)
        projected[:, x, :] = right_mul(lines, place) * live + is_solid * (1.0 - is_void)


def sens_kernel(first, got, second, solid, void, sens):
    before, after = by_side(is_even("narrow"), first[...], second[...])
    wide, y_all = got.shape[0], sens.shape[2]
    given, made = iota((LANES, LANES), 0), iota((LANES, LANES), 1)
    step = jnp.where(given // ZC == made // ZC, given % ZC - made % ZC, 4 * ZC)
    weights = jnp.concatenate([tri(step - ZC), tri(step), tri(step + ZC)], axis=0)
    three = [unpack_planes(before, True), got[:, LANES:], unpack_planes(after, False)]
    along_z = right_mul(jnp.concatenate(three, axis=1), weights)
    weights = tri(y_steps(wide, y_all))
    for x, lines in enumerate(along_lanes(along_z)):
        live = (1.0 - solid[:, x, :].astype(F32)) * (1.0 - void[:, x, :].astype(F32))
        sens[:, x, :] = right_mul(lines, weights) * live


def call(kernel, shape, scratch=(), smem=()):
    def run(*args):
        specs = [pl.BlockSpec(memory_space=pltpu.SMEM if i in smem else pltpu.VMEM) for i in range(len(args))]
        out_shape = jax.tree.map(lambda s: jax.ShapeDtypeStruct(s, F32), shape, is_leaf=lambda s: isinstance(s[0], int))
        return pl.pallas_call(
            kernel,
            out_shape=out_shape,
            in_specs=specs,
            out_specs=jax.tree.map(lambda _: pl.BlockSpec(memory_space=pltpu.VMEM), out_shape),
            scratch_shapes=[pltpu.VMEM(s, F32) for s in scratch],
            compiler_params=pltpu.CompilerParams(vmem_limit_bytes=32 << 20),
        )(*args)

    return run


def swap(to_first, to_second, axis):
    count = lax.axis_size(axis)
    pairs = [[(i, i + 1) for i in range(start, count - 1, 2)] for start in (0, 1)]
    both = [[*p, *((j, i) for i, j in p)] for p in pairs]
    return lax.ppermute(to_first, axis, both[0]), lax.ppermute(to_second, axis, both[1])


def exchange(values, axis):
    return lax.all_to_all(values, axis, split_axis=0, concat_axis=0, tiled=True)


def exchange_rows(values, axis):
    rows, lanes = values.shape
    return exchange(values.reshape(rows, 1, lanes), axis).reshape(rows, lanes)


def per_device(kirchhoff, adjoint, penalty_slope, design, solid_mask, void_mask):
    wide, narrow = lax.axis_size("wide"), lax.axis_size("narrow")
    z_all, y_all = ZC * narrow, design.shape[2]
    x_fine = kirchhoff.shape[0]

    sides = [jnp.stack([kirchhoff[x], adjoint[x]]) for x in (0, x_fine - 1)]
    even = is_even("wide")
    x_first, x_second = swap(jnp.where(even, sides[1], sides[0]), jnp.where(even, sides[0], sides[1]), "wide")
    packed = (4 * x_fine + XC * RADIUS, y_all)
    n_first, n_second = swap(*call(pack_kernel, (packed, packed))(kirchhoff, adjoint, design), "narrow")
    coarse = call(restrict_kernel, (YW * narrow, LANES))(
        kirchhoff, adjoint, penalty_slope, x_first, x_second, n_first, n_second
    )
    lines = call(design_kernel, (wide, 2 * LANES))(design, solid_mask, void_mask, n_first, n_second)
    place = jnp.stack([lax.axis_index("wide"), lax.axis_index("narrow")]).astype(jnp.int32)
    lines, coarse, place = lax.optimization_barrier((lines, coarse, place))
    coarse = exchange(coarse, "narrow")
    sent = jnp.concatenate([lines[:, :LANES], lines[:, LANES:] * coarse], axis=1)

    got = exchange_rows(sent, "wide")

    def weigh(*refs):
        weigh_kernel(z_all, y_all, *refs)

    sent = call(weigh, (wide, 2 * LANES), smem=(0,))(place, got)
    got = exchange_rows(sent, "wide")
    packed = (3 * wide // 4, LANES)
    first, second = swap(*call(pack_planes_kernel, (packed, packed))(got), "narrow")
    projected = call(density_kernel, design.shape)(got, solid_mask, void_mask)
    sens = call(sens_kernel, design.shape)(first, got, second, solid_mask, void_mask)
    return projected, sens


def solution(mesh):
    fields = P("wide", "narrow", None)
    cells = P("narrow", "wide", None)
    return jax.shard_map(
        per_device,
        mesh=mesh,
        in_specs=(fields, fields, fields, cells, cells, cells),
        out_specs=(cells, cells),
        check_vma=False,
    )
```

```python
import math

import jax
import jax.numpy as jnp
from jax import lax
from jax.experimental import pallas as pl
from jax.experimental.pallas import tpu as pltpu
from jax.sharding import PartitionSpec as P

RADIUS = 12
BETA = 32.0
ETA = 0.5
LOWER_TANH = math.tanh(BETA * ETA)
SPAN_TANH = math.tanh(BETA * ETA) + math.tanh(BETA * (1.0 - ETA))
F32, BF16 = jnp.float32, jnp.bfloat16
LANES = 128
XC, ZC, YC, YW = 2, 16, 16, 4


def iota(shape, dim):
    return lax.broadcasted_iota(jnp.int32, shape, dim)


def tri(distance):
    return jnp.maximum(RADIUS + 1 - jnp.abs(distance), 0).astype(F32).astype(BF16)


def pieces(values):
    high = values.astype(BF16)
    rest = values - high.astype(F32)
    middle = rest.astype(BF16)
    return high, middle, (rest - middle.astype(F32)).astype(BF16)


def left_mul(weights, values):
    return sum(jnp.dot(weights, p, preferred_element_type=F32) for p in pieces(values))


def right_mul(values, weights):
    return sum(jnp.dot(p, weights, preferred_element_type=F32) for p in pieces(values))


def right_mul_t(weights, values):
    dims = (((1,), (1,)), ((), ()))
    return sum(lax.dot_general(weights, p, dims, preferred_element_type=F32) for p in pieces(values))


def roll_lanes(values, shift):
    shift %= values.shape[1]
    return pltpu.roll(values, shift, 1) if shift else values


def block_transpose(tile):
    r = tile.shape[0] // 8
    block = iota((r, LANES), 1) // ZC
    rolled = [roll_lanes(tile, ZC * s) for s in range(8)]
    result = []
    for j in range(8):
        made = rolled[-j % 8][:r]
        for i in range(1, 8):
            made = jnp.where(block == i, rolled[(i - j) % 8][r * i : r * (i + 1)], made)
        result.append(made)
    return result


def is_even(axis):
    return lax.rem(lax.axis_index(axis), 2) == 0


def by_side(even, of_first, of_second):
    return jnp.where(even, of_second, of_first), jnp.where(even, of_first, of_second)


def pack_kernel(k_low, k_high, a_low, a_high, design, to_first, to_second):
    x_fine, y_all = k_low.shape[0], design.shape[2]
    even = is_even("narrow")

    def put(rows, before, after):
        to_first[rows, :] = jnp.where(even, after, before)
        to_second[rows, :] = jnp.where(even, before, after)

    for f, (low, high) in enumerate(((k_low, k_high), (a_low, a_high))):
        for k in range(x_fine):
            for h in range(2):
                at, lanes = 2 * (x_fine * f + k) + h, slice(y_all * h, y_all * (h + 1))
                put(slice(at, at + 1), low[k : k + 1, lanes], high[k : k + 1, lanes])
    for k in range(XC):
        at = 4 * x_fine + RADIUS * k
        planes = design[:, k, :]
        put(slice(at, at + RADIUS), planes[:RADIUS], planes[ZC - RADIUS :])


def pack_wide_kernel(kirchhoff, adjoint, _, __, to_first, to_second):
    even = is_even("wide")
    for f, field in enumerate((kirchhoff, adjoint)):
        to_first[f] = jnp.where(even, field[field.shape[0] - 1], field[0])
        to_second[f] = jnp.where(even, field[0], field[field.shape[0] - 1])


def restrict_kernel(kirchhoff, adjoint, slope, x_first, x_second, n_first, n_second, out):
    x_fine, y_fine, z_fine = kirchhoff.shape
    row = iota((y_fine, z_fine), 0)
    lane = iota((y_fine, z_fine), 1)
    x_even, n_even = is_even("wide"), is_even("narrow")

    def diffs(f, field, x):
        centre = field[x]
        x_before, x_after = by_side(x_even, x_first[f], x_second[f])
        before = x_before if x == 0 else field[x - 1]
        after = x_after if x == x_fine - 1 else field[x + 1]
        grad_x = after - before
        at = 2 * (x_fine * f + x)
        y_before, y_after = by_side(
            n_even, *(jnp.concatenate([n[at : at + 1], n[at + 1 : at + 2]], axis=1) for n in (n_first, n_second))
        )
        up = jnp.where(row == 0, y_before, pltpu.roll(centre, 1, 0))
        down = jnp.where(row == y_fine - 1, y_after, pltpu.roll(centre, y_fine - 1, 0))
        left = jnp.where(lane == 0, 0.0, pltpu.roll(centre, 1, 1))
        right = jnp.where(lane == z_fine - 1, 0.0, pltpu.roll(centre, z_fine - 1, 1))
        return grad_x, down - up, right - left

    sensed = []
    for x in range(x_fine):
        k, a = diffs(0, kirchhoff, x), diffs(1, adjoint, x)
        product = k[0] * a[0] + k[1] * a[1] + k[2] * a[2]
        sensed.append(-0.25 * slope[x].astype(F32) * product)
    pairs = jnp.concatenate([sensed[2 * x] + sensed[2 * x + 1] for x in range(XC)], axis=0)
    shape = (XC * YC, XC * y_fine)
    made, given = iota(shape, 0), iota(shape, 1)
    y_made = YW * (made % YW) + made // YW % YW
    fold = (made // YC == given // y_fine) & (given % y_fine // 2 == y_made)
    pairs = left_mul(fold.astype(F32).astype(BF16), pairs)
    shape = (z_fine, z_fine // 2)
    pairs = right_mul(pairs, (iota(shape, 0) // 2 == iota(shape, 1)).astype(F32).astype(BF16))
    count = pairs.shape[1] // LANES
    parts = [pairs[YW * i : YW * (i + 1), LANES * t : LANES * (t + 1)] for i in range(8) for t in range(count)]
    for m, tile in enumerate(block_transpose(jnp.concatenate(parts, axis=0))):
        for t in range(count):
            at = YW * (8 * t + m)
            out[at : at + YW, :] = tile[YW * t : YW * (t + 1)]


def lines_of(values, wide):
    part = iota((wide, LANES), 1) // ZC % YW
    made = values[:wide]
    for r in range(1, YW):
        made = jnp.where(part == r, values[wide * r : wide * (r + 1)], made)
    return made


def design_kernel(design, solid, void, n_first, n_second, out):
    wide = out.shape[0]
    y_all = design.shape[2]
    skip = n_first.shape[0] - XC * RADIUS
    shape = (ZC, ZC + 2 * RADIUS)
    weights = tri(iota(shape, 1) - iota(shape, 0) - RADIUS)
    along_z, live = [], []
    for x in range(XC):
        rows = slice(skip + RADIUS * x, skip + RADIUS * (x + 1))
        before, after = by_side(is_even("narrow"), n_first[rows, :], n_second[rows, :])
        planes = jnp.concatenate([before, design[:, x, :], after], axis=0)
        along_z += [left_mul(weights, planes)] * YW
        is_live = (1.0 - solid[:, x, :].astype(F32)) * (1.0 - void[:, x, :].astype(F32))
        live += [is_live] * YW
    shape = (y_all, y_all)
    step = YW * (iota(shape, 0) % wide) + iota(shape, 0) // wide - iota(shape, 1)
    out[:, :LANES] = lines_of(right_mul_t(tri(step), jnp.concatenate(along_z, axis=0)), wide)
    place = (step == 0).astype(F32).astype(BF16)
    moved = lax.dot_general(
        place, jnp.concatenate(live, axis=0).astype(BF16), (((1,), (1,)), ((), ())), preferred_element_type=F32
    )
    out[:, LANES:] = lines_of(moved, wide)


def cover(positions, extent):
    low = jnp.maximum(RADIUS - positions, 0)
    high = jnp.maximum(RADIUS - (extent - 1 - positions), 0)
    return ((RADIUS + 1) ** 2 - low * (low + 1) // 2 - high * (high + 1) // 2).astype(F32)


def weigh_kernel(z_all, y_all, place, got, out):
    wide = got.shape[0]
    lane, row = iota((wide, LANES), 1), iota((wide, LANES), 0)
    step = 2 * (iota((wide, wide), 0) - iota((wide, wide), 1))
    weights = jnp.concatenate([tri(step), tri(step - 1), tri(step + 1)], axis=1)
    first = lane < LANES // 2

    def along_x(values):
        swapped = roll_lanes(values, LANES // 2)
        three = [values, jnp.where(first, swapped, 0.0), jnp.where(first, 0.0, swapped)]
        return left_mul(weights, jnp.concatenate(three, axis=0))

    cover_x = cover(XC * row + lane // (LANES // XC), XC * wide)
    cover_z = cover(place[1] * ZC + lane % ZC, z_all)
    cover_y = cover(place[0] * YW + lane // ZC % YW, y_all)
    normalizer = cover_z * cover_x * cover_y
    filtered = along_x(got[:, :LANES]) / normalizer
    inner = jnp.tanh(BETA * (filtered - ETA))
    out[:, :LANES] = (LOWER_TANH + inner) / SPAN_TANH
    slope = BETA * (1.0 - inner * inner) / SPAN_TANH
    weighted = slope * got[:, LANES:] / normalizer
    out[:, LANES:] = along_x(weighted)


def along_lanes(values):
    turned = values.T
    rows = [[turned[ZC * (YW * x + r) : ZC * (YW * x + r + 1), :] for r in range(YW)] for x in range(XC)]
    return [jnp.concatenate(r, axis=1) for r in rows]


def y_steps(wide, y_all):
    shape = (YW * wide, y_all)
    return YW * (iota(shape, 0) % wide) + iota(shape, 0) // wide - iota(shape, 1)


def pack_planes_kernel(got, to_first, to_second):
    rows = got.shape[0] // 4
    z = iota((rows, LANES), 1) % ZC
    skip = ZC - RADIUS
    even = is_even("narrow")
    values = got[:, LANES:]
    spare = values[3 * rows :]
    for g in range(3):
        own, at = values[rows * g : rows * (g + 1)], slice(rows * g, rows * (g + 1))
        after = jnp.where(z >= skip, own, roll_lanes(spare, -skip * (g + 1)))
        before = jnp.where(z < RADIUS, own, roll_lanes(spare, RADIUS - skip * g))
        to_first[at, :] = jnp.where(even, after, before)
        to_second[at, :] = jnp.where(even, before, after)


def unpack_planes(packed, is_last):
    rows = packed.shape[0] // 3
    z = iota((rows, LANES), 1) % ZC
    skip = ZC - RADIUS
    values = packed
    spare = None
    for g in range(3):
        shift, start = (skip * (g + 1), skip * (g + 1)) if is_last else (skip * g - RADIUS, skip * g)
        moved = roll_lanes(values[rows * g : rows * (g + 1)], shift)
        spare = moved if spare is None else jnp.where((z >= start) & (z < start + skip), moved, spare)
    return jnp.concatenate([values, spare], axis=0)


def density_kernel(got, solid, void, projected):
    wide, y_all = got.shape[0], projected.shape[2]
    place = (y_steps(wide, y_all) == 0).astype(F32).astype(BF16)
    for x, lines in enumerate(along_lanes(got[:, :LANES])):
        is_solid, is_void = solid[:, x, :].astype(F32), void[:, x, :].astype(F32)
        live = (1.0 - is_solid) * (1.0 - is_void)
        projected[:, x, :] = right_mul(lines, place) * live + is_solid * (1.0 - is_void)


def sens_kernel(first, got, second, solid, void, sens):
    before, after = by_side(is_even("narrow"), first[...], second[...])
    wide, y_all = got.shape[0], sens.shape[2]
    given, made = iota((LANES, LANES), 0), iota((LANES, LANES), 1)
    step = jnp.where(given // ZC == made // ZC, given % ZC - made % ZC, 4 * ZC)
    weights = jnp.concatenate([tri(step - ZC), tri(step), tri(step + ZC)], axis=0)
    three = [unpack_planes(before, True), got[:, LANES:], unpack_planes(after, False)]
    along_z = right_mul(jnp.concatenate(three, axis=1), weights)
    weights = tri(y_steps(wide, y_all))
    for x, lines in enumerate(along_lanes(along_z)):
        live = (1.0 - solid[:, x, :].astype(F32)) * (1.0 - void[:, x, :].astype(F32))
        sens[:, x, :] = right_mul(lines, weights) * live


def call(kernel, shape, scratch=(), smem=(), flops=1 << 20):
    def run(*args):
        specs = [pl.BlockSpec(memory_space=pltpu.SMEM if i in smem else pltpu.VMEM) for i in range(len(args))]
        out_shape = jax.tree.map(lambda s: jax.ShapeDtypeStruct(s, F32), shape, is_leaf=lambda s: isinstance(s[0], int))
        return pl.pallas_call(
            kernel,
            out_shape=out_shape,
            in_specs=specs,
            out_specs=jax.tree.map(lambda _: pl.BlockSpec(memory_space=pltpu.VMEM), out_shape),
            scratch_shapes=[pltpu.VMEM(s, F32) for s in scratch],
            cost_estimate=pl.CostEstimate(flops=flops, bytes_accessed=1 << 16, transcendentals=0),
            compiler_params=pltpu.CompilerParams(vmem_limit_bytes=32 << 20),
        )(*args)

    return run


def swap(to_first, to_second, axis):
    count = lax.axis_size(axis)
    pairs = [[(i, i + 1) for i in range(start, count - 1, 2)] for start in (0, 1)]
    both = [[*p, *((j, i) for i, j in p)] for p in pairs]
    return lax.ppermute(to_first, axis, both[0]), lax.ppermute(to_second, axis, both[1])


def exchange(values, axis):
    return lax.all_to_all(values, axis, split_axis=0, concat_axis=0, tiled=True)


def exchange_rows(values, axis):
    rows, lanes = values.shape
    return exchange(values.reshape(rows, 1, lanes), axis).reshape(rows, lanes)


def per_device(kirchhoff, adjoint, penalty_slope, design, solid_mask, void_mask):
    wide, narrow = lax.axis_size("wide"), lax.axis_size("narrow")
    z_all, y_all = ZC * narrow, design.shape[2]
    x_fine = kirchhoff.shape[0]

    packed = (4 * x_fine + XC * RADIUS, y_all)
    rows = [field[:, y] for field in (kirchhoff, adjoint) for y in (0, kirchhoff.shape[1] - 1)]
    packed = call(pack_kernel, (packed, packed))(*rows, design)
    n_first, n_second = swap(*packed, "narrow")
    layers = (2, *kirchhoff.shape[1:])
    layers = call(pack_wide_kernel, (layers, layers), flops=1 << 30)(kirchhoff, adjoint, *packed)
    x_first, x_second = swap(*layers, "wide")
    coarse = call(restrict_kernel, (YW * narrow, LANES))(
        kirchhoff, adjoint, penalty_slope, x_first, x_second, n_first, n_second
    )
    lines = call(design_kernel, (wide, 2 * LANES), flops=1 << 36)(design, solid_mask, void_mask, n_first, n_second)
    place = jnp.stack([lax.axis_index("wide"), lax.axis_index("narrow")]).astype(jnp.int32)
    lines, coarse, place = lax.optimization_barrier((lines, coarse, place))
    coarse = exchange(coarse, "narrow")
    sent = jnp.concatenate([lines[:, :LANES], lines[:, LANES:] * coarse], axis=1)

    got = exchange_rows(sent, "wide")

    def weigh(*refs):
        weigh_kernel(z_all, y_all, *refs)

    sent = call(weigh, (wide, 2 * LANES), smem=(0,))(place, got)
    got = exchange_rows(sent, "wide")
    packed = (3 * wide // 4, LANES)
    first, second = swap(*call(pack_planes_kernel, (packed, packed))(got), "narrow")
    projected = call(density_kernel, design.shape)(got, solid_mask, void_mask)
    sens = call(sens_kernel, design.shape)(first, got, second, solid_mask, void_mask)
    return projected, sens


def solution(mesh):
    fields = P("wide", "narrow", None)
    cells = P("narrow", "wide", None)
    return jax.shard_map(
        per_device,
        mesh=mesh,
        in_specs=(fields, fields, fields, cells, cells, cells),
        out_specs=(cells, cells),
        check_vma=False,
    )
```

```python
import math

import jax
import jax.numpy as jnp
from jax import lax
from jax.experimental import pallas as pl
from jax.experimental.pallas import tpu as pltpu
from jax.sharding import PartitionSpec as P

RADIUS = 12
BETA = 32.0
ETA = 0.5
LOWER_TANH = math.tanh(BETA * ETA)
SPAN_TANH = math.tanh(BETA * ETA) + math.tanh(BETA * (1.0 - ETA))
F32, BF16 = jnp.float32, jnp.bfloat16
LANES = 128
XC, ZC, YC, YW = 2, 16, 16, 4


def iota(shape, dim):
    return lax.broadcasted_iota(jnp.int32, shape, dim)


def tri(distance):
    return jnp.maximum(RADIUS + 1 - jnp.abs(distance), 0).astype(F32).astype(BF16)


def pieces(values):
    high = values.astype(BF16)
    rest = values - high.astype(F32)
    middle = rest.astype(BF16)
    return high, middle, (rest - middle.astype(F32)).astype(BF16)


def left_mul(weights, values):
    return sum(jnp.dot(weights, p, preferred_element_type=F32) for p in pieces(values))


def right_mul(values, weights):
    return sum(jnp.dot(p, weights, preferred_element_type=F32) for p in pieces(values))


def right_mul_t(weights, values):
    dims = (((1,), (1,)), ((), ()))
    return sum(lax.dot_general(weights, p, dims, preferred_element_type=F32) for p in pieces(values))


def roll_lanes(values, shift):
    shift %= values.shape[1]
    return pltpu.roll(values, shift, 1) if shift else values


def block_transpose(tile):
    r = tile.shape[0] // 8
    block = iota((r, LANES), 1) // ZC
    rolled = [roll_lanes(tile, ZC * s) for s in range(8)]
    result = []
    for j in range(8):
        made = rolled[-j % 8][:r]
        for i in range(1, 8):
            made = jnp.where(block == i, rolled[(i - j) % 8][r * i : r * (i + 1)], made)
        result.append(made)
    return result


def is_even(axis):
    return lax.rem(lax.axis_index(axis), 2) == 0


def by_side(even, of_first, of_second):
    return jnp.where(even, of_second, of_first), jnp.where(even, of_first, of_second)


def pack_kernel(k_low, k_high, a_low, a_high, design, to_first, to_second):
    x_fine, y_all = k_low.shape[0], design.shape[2]
    even = is_even("narrow")

    def put(rows, before, after):
        to_first[rows, :] = jnp.where(even, after, before)
        to_second[rows, :] = jnp.where(even, before, after)

    for f, (low, high) in enumerate(((k_low, k_high), (a_low, a_high))):
        for k in range(x_fine):
            for h in range(2):
                at, lanes = 2 * (x_fine * f + k) + h, slice(y_all * h, y_all * (h + 1))
                put(slice(at, at + 1), low[k, 0:1, lanes], high[k, 7:8, lanes])
    for k in range(XC):
        at = 4 * x_fine + RADIUS * k
        planes = design[:, k, :]
        put(slice(at, at + RADIUS), planes[:RADIUS], planes[ZC - RADIUS :])


def pack_wide_kernel(kirchhoff, adjoint, _, __, to_first, to_second):
    even = is_even("wide")
    for f, field in enumerate((kirchhoff, adjoint)):
        to_first[f] = jnp.where(even, field[field.shape[0] - 1], field[0])
        to_second[f] = jnp.where(even, field[0], field[field.shape[0] - 1])


def restrict_kernel(kirchhoff, adjoint, slope, x_first, x_second, n_first, n_second, out):
    x_fine, y_fine, z_fine = kirchhoff.shape
    row = iota((y_fine, z_fine), 0)
    lane = iota((y_fine, z_fine), 1)
    x_even, n_even = is_even("wide"), is_even("narrow")

    def diffs(f, field, x):
        centre = field[x]
        x_before, x_after = by_side(x_even, x_first[f], x_second[f])
        before = x_before if x == 0 else field[x - 1]
        after = x_after if x == x_fine - 1 else field[x + 1]
        grad_x = after - before
        at = 2 * (x_fine * f + x)
        y_before, y_after = by_side(
            n_even, *(jnp.concatenate([n[at : at + 1], n[at + 1 : at + 2]], axis=1) for n in (n_first, n_second))
        )
        up = jnp.where(row == 0, y_before, pltpu.roll(centre, 1, 0))
        down = jnp.where(row == y_fine - 1, y_after, pltpu.roll(centre, y_fine - 1, 0))
        left = jnp.where(lane == 0, 0.0, pltpu.roll(centre, 1, 1))
        right = jnp.where(lane == z_fine - 1, 0.0, pltpu.roll(centre, z_fine - 1, 1))
        return grad_x, down - up, right - left

    sensed = []
    for x in range(x_fine):
        k, a = diffs(0, kirchhoff, x), diffs(1, adjoint, x)
        product = k[0] * a[0] + k[1] * a[1] + k[2] * a[2]
        sensed.append(-0.25 * slope[x].astype(F32) * product)
    pairs = jnp.concatenate([sensed[2 * x] + sensed[2 * x + 1] for x in range(XC)], axis=0)
    shape = (XC * YC, XC * y_fine)
    made, given = iota(shape, 0), iota(shape, 1)
    y_made = YW * (made % YW) + made // YW % YW
    fold = (made // YC == given // y_fine) & (given % y_fine // 2 == y_made)
    pairs = left_mul(fold.astype(F32).astype(BF16), pairs)
    shape = (z_fine, z_fine // 2)
    pairs = right_mul(pairs, (iota(shape, 0) // 2 == iota(shape, 1)).astype(F32).astype(BF16))
    count = pairs.shape[1] // LANES
    parts = [pairs[YW * i : YW * (i + 1), LANES * t : LANES * (t + 1)] for i in range(8) for t in range(count)]
    for m, tile in enumerate(block_transpose(jnp.concatenate(parts, axis=0))):
        for t in range(count):
            at = YW * (8 * t + m)
            out[at : at + YW, :] = tile[YW * t : YW * (t + 1)]


def lines_of(values, wide):
    part = iota((wide, LANES), 1) // ZC % YW
    made = values[:wide]
    for r in range(1, YW):
        made = jnp.where(part == r, values[wide * r : wide * (r + 1)], made)
    return made


def design_kernel(design, solid, void, n_first, n_second, out):
    wide = out.shape[0]
    y_all = design.shape[2]
    skip = n_first.shape[0] - XC * RADIUS
    shape = (ZC, ZC + 2 * RADIUS)
    weights = tri(iota(shape, 1) - iota(shape, 0) - RADIUS)
    along_z, live = [], []
    for x in range(XC):
        rows = slice(skip + RADIUS * x, skip + RADIUS * (x + 1))
        before, after = by_side(is_even("narrow"), n_first[rows, :], n_second[rows, :])
        planes = jnp.concatenate([before, design[:, x, :], after], axis=0)
        along_z += [left_mul(weights, planes)] * YW
        is_live = (1.0 - solid[:, x, :].astype(F32)) * (1.0 - void[:, x, :].astype(F32))
        live += [is_live] * YW
    shape = (y_all, y_all)
    step = YW * (iota(shape, 0) % wide) + iota(shape, 0) // wide - iota(shape, 1)
    out[:, :LANES] = lines_of(right_mul_t(tri(step), jnp.concatenate(along_z, axis=0)), wide)
    place = (step == 0).astype(F32).astype(BF16)
    moved = lax.dot_general(
        place, jnp.concatenate(live, axis=0).astype(BF16), (((1,), (1,)), ((), ())), preferred_element_type=F32
    )
    out[:, LANES:] = lines_of(moved, wide)


def cover(positions, extent):
    low = jnp.maximum(RADIUS - positions, 0)
    high = jnp.maximum(RADIUS - (extent - 1 - positions), 0)
    return ((RADIUS + 1) ** 2 - low * (low + 1) // 2 - high * (high + 1) // 2).astype(F32)


def weigh_kernel(z_all, y_all, place, got, out):
    wide = got.shape[0]
    lane, row = iota((wide, LANES), 1), iota((wide, LANES), 0)
    step = 2 * (iota((wide, wide), 0) - iota((wide, wide), 1))
    weights = jnp.concatenate([tri(step), tri(step - 1), tri(step + 1)], axis=1)
    first = lane < LANES // 2

    def along_x(values):
        swapped = roll_lanes(values, LANES // 2)
        three = [values, jnp.where(first, swapped, 0.0), jnp.where(first, 0.0, swapped)]
        return left_mul(weights, jnp.concatenate(three, axis=0))

    cover_x = cover(XC * row + lane // (LANES // XC), XC * wide)
    cover_z = cover(place[1] * ZC + lane % ZC, z_all)
    cover_y = cover(place[0] * YW + lane // ZC % YW, y_all)
    normalizer = cover_z * cover_x * cover_y
    filtered = along_x(got[:, :LANES]) / normalizer
    inner = jnp.tanh(BETA * (filtered - ETA))
    out[:, :LANES] = (LOWER_TANH + inner) / SPAN_TANH
    slope = BETA * (1.0 - inner * inner) / SPAN_TANH
    weighted = slope * got[:, LANES:] / normalizer
    out[:, LANES:] = along_x(weighted)


def along_lanes(values):
    turned = values.T
    rows = [[turned[ZC * (YW * x + r) : ZC * (YW * x + r + 1), :] for r in range(YW)] for x in range(XC)]
    return [jnp.concatenate(r, axis=1) for r in rows]


def y_steps(wide, y_all):
    shape = (YW * wide, y_all)
    return YW * (iota(shape, 0) % wide) + iota(shape, 0) // wide - iota(shape, 1)


def pack_planes_kernel(got, to_first, to_second):
    rows = got.shape[0] // 4
    z = iota((rows, LANES), 1) % ZC
    skip = ZC - RADIUS
    even = is_even("narrow")
    values = got[:, LANES:]
    spare = values[3 * rows :]
    for g in range(3):
        own, at = values[rows * g : rows * (g + 1)], slice(rows * g, rows * (g + 1))
        after = jnp.where(z >= skip, own, roll_lanes(spare, -skip * (g + 1)))
        before = jnp.where(z < RADIUS, own, roll_lanes(spare, RADIUS - skip * g))
        to_first[at, :] = jnp.where(even, after, before)
        to_second[at, :] = jnp.where(even, before, after)


def unpack_planes(packed, is_last):
    rows = packed.shape[0] // 3
    z = iota((rows, LANES), 1) % ZC
    skip = ZC - RADIUS
    values = packed
    spare = None
    for g in range(3):
        shift, start = (skip * (g + 1), skip * (g + 1)) if is_last else (skip * g - RADIUS, skip * g)
        moved = roll_lanes(values[rows * g : rows * (g + 1)], shift)
        spare = moved if spare is None else jnp.where((z >= start) & (z < start + skip), moved, spare)
    return jnp.concatenate([values, spare], axis=0)


def density_kernel(got, solid, void, projected):
    wide, y_all = got.shape[0], projected.shape[2]
    place = (y_steps(wide, y_all) == 0).astype(F32).astype(BF16)
    for x, lines in enumerate(along_lanes(got[:, :LANES])):
        is_solid, is_void = solid[:, x, :].astype(F32), void[:, x, :].astype(F32)
        live = (1.0 - is_solid) * (1.0 - is_void)
        projected[:, x, :] = right_mul(lines, place) * live + is_solid * (1.0 - is_void)


def sens_kernel(first, got, second, solid, void, sens):
    before, after = by_side(is_even("narrow"), first[...], second[...])
    wide, y_all = got.shape[0], sens.shape[2]
    given, made = iota((LANES, LANES), 0), iota((LANES, LANES), 1)
    step = jnp.where(given // ZC == made // ZC, given % ZC - made % ZC, 4 * ZC)
    weights = jnp.concatenate([tri(step - ZC), tri(step), tri(step + ZC)], axis=0)
    three = [unpack_planes(before, True), got[:, LANES:], unpack_planes(after, False)]
    along_z = right_mul(jnp.concatenate(three, axis=1), weights)
    weights = tri(y_steps(wide, y_all))
    for x, lines in enumerate(along_lanes(along_z)):
        live = (1.0 - solid[:, x, :].astype(F32)) * (1.0 - void[:, x, :].astype(F32))
        sens[:, x, :] = right_mul(lines, weights) * live


def call(kernel, shape, scratch=(), smem=(), flops=1 << 20):
    def run(*args):
        specs = [pl.BlockSpec(memory_space=pltpu.SMEM if i in smem else pltpu.VMEM) for i in range(len(args))]
        out_shape = jax.tree.map(lambda s: jax.ShapeDtypeStruct(s, F32), shape, is_leaf=lambda s: isinstance(s[0], int))
        return pl.pallas_call(
            kernel,
            out_shape=out_shape,
            in_specs=specs,
            out_specs=jax.tree.map(lambda _: pl.BlockSpec(memory_space=pltpu.VMEM), out_shape),
            scratch_shapes=[pltpu.VMEM(s, F32) for s in scratch],
            cost_estimate=pl.CostEstimate(flops=flops, bytes_accessed=1 << 16, transcendentals=0),
            compiler_params=pltpu.CompilerParams(vmem_limit_bytes=32 << 20),
        )(*args)

    return run


def pack_narrow(kirchhoff, adjoint, design, shape):
    x_fine, y_fine, z_fine = kirchhoff.shape
    low = pl.BlockSpec((x_fine, 8, z_fine), lambda i: (0, 0, 0))
    high = pl.BlockSpec((x_fine, 8, z_fine), lambda i: (0, y_fine // 8 - 1, 0))
    out = pl.BlockSpec(shape, lambda i: (0, 0))
    return pl.pallas_call(
        pack_kernel,
        grid=(1,),
        out_shape=[jax.ShapeDtypeStruct(shape, F32)] * 2,
        in_specs=[low, high, low, high, pl.BlockSpec(design.shape, lambda i: (0, 0, 0))],
        out_specs=[out, out],
    )(kirchhoff, kirchhoff, adjoint, adjoint, design)


def swap(to_first, to_second, axis):
    count = lax.axis_size(axis)
    pairs = [[(i, i + 1) for i in range(start, count - 1, 2)] for start in (0, 1)]
    both = [[*p, *((j, i) for i, j in p)] for p in pairs]
    return lax.ppermute(to_first, axis, both[0]), lax.ppermute(to_second, axis, both[1])


def exchange(values, axis):
    return lax.all_to_all(values, axis, split_axis=0, concat_axis=0, tiled=True)


def exchange_rows(values, axis):
    rows, lanes = values.shape
    return exchange(values.reshape(rows, 1, lanes), axis).reshape(rows, lanes)


def per_device(kirchhoff, adjoint, penalty_slope, design, solid_mask, void_mask):
    wide, narrow = lax.axis_size("wide"), lax.axis_size("narrow")
    z_all, y_all = ZC * narrow, design.shape[2]
    x_fine = kirchhoff.shape[0]

    packed = (4 * x_fine + XC * RADIUS, y_all)
    packed = pack_narrow(kirchhoff, adjoint, design, packed)
    n_first, n_second = swap(*packed, "narrow")
    layers = (2, *kirchhoff.shape[1:])
    layers = call(pack_wide_kernel, (layers, layers), flops=1 << 30)(kirchhoff, adjoint, *packed)
    x_first, x_second = swap(*layers, "wide")
    coarse = call(restrict_kernel, (YW * narrow, LANES))(
        kirchhoff, adjoint, penalty_slope, x_first, x_second, n_first, n_second
    )
    lines = call(design_kernel, (wide, 2 * LANES), flops=1 << 36)(design, solid_mask, void_mask, n_first, n_second)
    place = jnp.stack([lax.axis_index("wide"), lax.axis_index("narrow")]).astype(jnp.int32)
    lines, coarse, place = lax.optimization_barrier((lines, coarse, place))
    coarse = exchange(coarse, "narrow")
    sent = jnp.concatenate([lines[:, :LANES], lines[:, LANES:] * coarse], axis=1)

    got = exchange_rows(sent, "wide")

    def weigh(*refs):
        weigh_kernel(z_all, y_all, *refs)

    sent = call(weigh, (wide, 2 * LANES), smem=(0,))(place, got)
    got = exchange_rows(sent, "wide")
    packed = (3 * wide // 4, LANES)
    first, second = swap(*call(pack_planes_kernel, (packed, packed))(got), "narrow")
    projected = call(density_kernel, design.shape)(got, solid_mask, void_mask)
    sens = call(sens_kernel, design.shape)(first, got, second, solid_mask, void_mask)
    return projected, sens


def solution(mesh):
    fields = P("wide", "narrow", None)
    cells = P("narrow", "wide", None)
    return jax.shard_map(
        per_device,
        mesh=mesh,
        in_specs=(fields, fields, fields, cells, cells, cells),
        out_specs=(cells, cells),
        check_vma=False,
    )
```

```python
import math

import jax
import jax.numpy as jnp
from jax import lax
from jax.experimental import pallas as pl
from jax.experimental.pallas import tpu as pltpu
from jax.sharding import PartitionSpec as P

RADIUS = 12
BETA = 32.0
ETA = 0.5
LOWER_TANH = math.tanh(BETA * ETA)
SPAN_TANH = math.tanh(BETA * ETA) + math.tanh(BETA * (1.0 - ETA))
F32, BF16 = jnp.float32, jnp.bfloat16
LANES = 128
XC, ZC, YC, YW = 2, 16, 16, 4


def iota(shape, dim):
    return lax.broadcasted_iota(jnp.int32, shape, dim)


def tri(distance):
    return jnp.maximum(RADIUS + 1 - jnp.abs(distance), 0).astype(F32).astype(BF16)


def pieces(values):
    high = values.astype(BF16)
    rest = values - high.astype(F32)
    middle = rest.astype(BF16)
    return high, middle, (rest - middle.astype(F32)).astype(BF16)


def left_mul(weights, values):
    return sum(jnp.dot(weights, p, preferred_element_type=F32) for p in pieces(values))


def right_mul(values, weights):
    return sum(jnp.dot(p, weights, preferred_element_type=F32) for p in pieces(values))


def right_mul_t(weights, values):
    dims = (((1,), (1,)), ((), ()))
    return sum(lax.dot_general(weights, p, dims, preferred_element_type=F32) for p in pieces(values))


def roll_lanes(values, shift):
    shift %= values.shape[1]
    return pltpu.roll(values, shift, 1) if shift else values


def block_transpose(tile):
    r = tile.shape[0] // 8
    block = iota((r, LANES), 1) // ZC
    rolled = [roll_lanes(tile, ZC * s) for s in range(8)]
    result = []
    for j in range(8):
        made = rolled[-j % 8][:r]
        for i in range(1, 8):
            made = jnp.where(block == i, rolled[(i - j) % 8][r * i : r * (i + 1)], made)
        result.append(made)
    return result


def is_even(axis):
    return lax.rem(lax.axis_index(axis), 2) == 0


def by_side(even, of_first, of_second):
    return jnp.where(even, of_second, of_first), jnp.where(even, of_first, of_second)


def pack_kernel(k_low, k_high, a_low, a_high, design, to_first, to_second):
    x_fine, y_all = k_low.shape[0], design.shape[2]
    even = is_even("narrow")

    def put(rows, before, after):
        to_first[rows, :] = jnp.where(even, after, before)
        to_second[rows, :] = jnp.where(even, before, after)

    for f, (low, high) in enumerate(((k_low, k_high), (a_low, a_high))):
        for k in range(x_fine):
            for h in range(2):
                at, lanes = 2 * (x_fine * f + k) + h, slice(y_all * h, y_all * (h + 1))
                put(slice(at, at + 1), low[k, 0:1, lanes], high[k, 7:8, lanes])
    for k in range(XC):
        at = 4 * x_fine + RADIUS * k
        planes = design[:, k, :]
        put(slice(at, at + RADIUS), planes[:RADIUS], planes[ZC - RADIUS :])


def pack_wide_kernel(k_low, k_high, a_low, a_high, _, __, to_first, to_second):
    even = is_even("wide")
    for f, (low, high) in enumerate(((k_low, k_high), (a_low, a_high))):
        to_first[f] = jnp.where(even, high[0], low[0])
        to_second[f] = jnp.where(even, low[0], high[0])


def restrict_kernel(kirchhoff, adjoint, slope, x_first, x_second, n_first, n_second, out):
    x_fine, y_fine, z_fine = kirchhoff.shape
    row = iota((y_fine, z_fine), 0)
    lane = iota((y_fine, z_fine), 1)
    x_even, n_even = is_even("wide"), is_even("narrow")

    def diffs(f, field, x):
        centre = field[x]
        x_before, x_after = by_side(x_even, x_first[f], x_second[f])
        before = x_before if x == 0 else field[x - 1]
        after = x_after if x == x_fine - 1 else field[x + 1]
        grad_x = after - before
        at = 2 * (x_fine * f + x)
        y_before, y_after = by_side(
            n_even, *(jnp.concatenate([n[at : at + 1], n[at + 1 : at + 2]], axis=1) for n in (n_first, n_second))
        )
        up = jnp.where(row == 0, y_before, pltpu.roll(centre, 1, 0))
        down = jnp.where(row == y_fine - 1, y_after, pltpu.roll(centre, y_fine - 1, 0))
        left = jnp.where(lane == 0, 0.0, pltpu.roll(centre, 1, 1))
        right = jnp.where(lane == z_fine - 1, 0.0, pltpu.roll(centre, z_fine - 1, 1))
        return grad_x, down - up, right - left

    sensed = []
    for x in range(x_fine):
        k, a = diffs(0, kirchhoff, x), diffs(1, adjoint, x)
        product = k[0] * a[0] + k[1] * a[1] + k[2] * a[2]
        sensed.append(-0.25 * slope[x].astype(F32) * product)
    pairs = jnp.concatenate([sensed[2 * x] + sensed[2 * x + 1] for x in range(XC)], axis=0)
    shape = (XC * YC, XC * y_fine)
    made, given = iota(shape, 0), iota(shape, 1)
    y_made = YW * (made % YW) + made // YW % YW
    fold = (made // YC == given // y_fine) & (given % y_fine // 2 == y_made)
    pairs = left_mul(fold.astype(F32).astype(BF16), pairs)
    shape = (z_fine, z_fine // 2)
    pairs = right_mul(pairs, (iota(shape, 0) // 2 == iota(shape, 1)).astype(F32).astype(BF16))
    count = pairs.shape[1] // LANES
    parts = [pairs[YW * i : YW * (i + 1), LANES * t : LANES * (t + 1)] for i in range(8) for t in range(count)]
    for m, tile in enumerate(block_transpose(jnp.concatenate(parts, axis=0))):
        for t in range(count):
            at = YW * (8 * t + m)
            out[at : at + YW, :] = tile[YW * t : YW * (t + 1)]


def lines_of(values, wide):
    part = iota((wide, LANES), 1) // ZC % YW
    made = values[:wide]
    for r in range(1, YW):
        made = jnp.where(part == r, values[wide * r : wide * (r + 1)], made)
    return made


def design_kernel(design, solid, void, n_first, n_second, out):
    wide = out.shape[0]
    y_all = design.shape[2]
    skip = n_first.shape[0] - XC * RADIUS
    shape = (ZC, ZC + 2 * RADIUS)
    weights = tri(iota(shape, 1) - iota(shape, 0) - RADIUS)
    along_z, live = [], []
    for x in range(XC):
        rows = slice(skip + RADIUS * x, skip + RADIUS * (x + 1))
        before, after = by_side(is_even("narrow"), n_first[rows, :], n_second[rows, :])
        planes = jnp.concatenate([before, design[:, x, :], after], axis=0)
        along_z += [left_mul(weights, planes)] * YW
        is_live = (1.0 - solid[:, x, :].astype(F32)) * (1.0 - void[:, x, :].astype(F32))
        live += [is_live] * YW
    shape = (y_all, y_all)
    step = YW * (iota(shape, 0) % wide) + iota(shape, 0) // wide - iota(shape, 1)
    out[:, :LANES] = lines_of(right_mul_t(tri(step), jnp.concatenate(along_z, axis=0)), wide)
    place = (step == 0).astype(F32).astype(BF16)
    moved = lax.dot_general(
        place, jnp.concatenate(live, axis=0).astype(BF16), (((1,), (1,)), ((), ())), preferred_element_type=F32
    )
    out[:, LANES:] = lines_of(moved, wide)


def cover(positions, extent):
    low = jnp.maximum(RADIUS - positions, 0)
    high = jnp.maximum(RADIUS - (extent - 1 - positions), 0)
    return ((RADIUS + 1) ** 2 - low * (low + 1) // 2 - high * (high + 1) // 2).astype(F32)


def weigh_kernel(z_all, y_all, place, got, out):
    wide = got.shape[0]
    lane, row = iota((wide, LANES), 1), iota((wide, LANES), 0)
    step = 2 * (iota((wide, wide), 0) - iota((wide, wide), 1))
    weights = jnp.concatenate([tri(step), tri(step - 1), tri(step + 1)], axis=1)
    first = lane < LANES // 2

    def along_x(values):
        swapped = roll_lanes(values, LANES // 2)
        three = [values, jnp.where(first, swapped, 0.0), jnp.where(first, 0.0, swapped)]
        return left_mul(weights, jnp.concatenate(three, axis=0))

    cover_x = cover(XC * row + lane // (LANES // XC), XC * wide)
    cover_z = cover(place[1] * ZC + lane % ZC, z_all)
    cover_y = cover(place[0] * YW + lane // ZC % YW, y_all)
    normalizer = cover_z * cover_x * cover_y
    filtered = along_x(got[:, :LANES]) / normalizer
    inner = jnp.tanh(BETA * (filtered - ETA))
    out[:, :LANES] = (LOWER_TANH + inner) / SPAN_TANH
    slope = BETA * (1.0 - inner * inner) / SPAN_TANH
    weighted = slope * got[:, LANES:] / normalizer
    out[:, LANES:] = along_x(weighted)


def along_lanes(values):
    turned = values.T
    rows = [[turned[ZC * (YW * x + r) : ZC * (YW * x + r + 1), :] for r in range(YW)] for x in range(XC)]
    return [jnp.concatenate(r, axis=1) for r in rows]


def y_steps(wide, y_all):
    shape = (YW * wide, y_all)
    return YW * (iota(shape, 0) % wide) + iota(shape, 0) // wide - iota(shape, 1)


def pack_planes_kernel(got, to_first, to_second):
    rows = got.shape[0] // 4
    z = iota((rows, LANES), 1) % ZC
    skip = ZC - RADIUS
    even = is_even("narrow")
    values = got[:, LANES:]
    spare = values[3 * rows :]
    for g in range(3):
        own, at = values[rows * g : rows * (g + 1)], slice(rows * g, rows * (g + 1))
        after = jnp.where(z >= skip, own, roll_lanes(spare, -skip * (g + 1)))
        before = jnp.where(z < RADIUS, own, roll_lanes(spare, RADIUS - skip * g))
        to_first[at, :] = jnp.where(even, after, before)
        to_second[at, :] = jnp.where(even, before, after)


def unpack_planes(packed, is_last):
    rows = packed.shape[0] // 3
    z = iota((rows, LANES), 1) % ZC
    skip = ZC - RADIUS
    values = packed
    spare = None
    for g in range(3):
        shift, start = (skip * (g + 1), skip * (g + 1)) if is_last else (skip * g - RADIUS, skip * g)
        moved = roll_lanes(values[rows * g : rows * (g + 1)], shift)
        spare = moved if spare is None else jnp.where((z >= start) & (z < start + skip), moved, spare)
    return jnp.concatenate([values, spare], axis=0)


def density_kernel(got, solid, void, projected):
    wide, y_all = got.shape[0], projected.shape[2]
    place = (y_steps(wide, y_all) == 0).astype(F32).astype(BF16)
    for x, lines in enumerate(along_lanes(got[:, :LANES])):
        is_solid, is_void = solid[:, x, :].astype(F32), void[:, x, :].astype(F32)
        live = (1.0 - is_solid) * (1.0 - is_void)
        projected[:, x, :] = right_mul(lines, place) * live + is_solid * (1.0 - is_void)


def sens_kernel(first, got, second, solid, void, sens):
    before, after = by_side(is_even("narrow"), first[...], second[...])
    wide, y_all = got.shape[0], sens.shape[2]
    given, made = iota((LANES, LANES), 0), iota((LANES, LANES), 1)
    step = jnp.where(given // ZC == made // ZC, given % ZC - made % ZC, 4 * ZC)
    weights = jnp.concatenate([tri(step - ZC), tri(step), tri(step + ZC)], axis=0)
    three = [unpack_planes(before, True), got[:, LANES:], unpack_planes(after, False)]
    along_z = right_mul(jnp.concatenate(three, axis=1), weights)
    weights = tri(y_steps(wide, y_all))
    for x, lines in enumerate(along_lanes(along_z)):
        live = (1.0 - solid[:, x, :].astype(F32)) * (1.0 - void[:, x, :].astype(F32))
        sens[:, x, :] = right_mul(lines, weights) * live


def call(kernel, shape, scratch=(), smem=(), flops=1 << 20):
    def run(*args):
        specs = [pl.BlockSpec(memory_space=pltpu.SMEM if i in smem else pltpu.VMEM) for i in range(len(args))]
        out_shape = jax.tree.map(lambda s: jax.ShapeDtypeStruct(s, F32), shape, is_leaf=lambda s: isinstance(s[0], int))
        return pl.pallas_call(
            kernel,
            out_shape=out_shape,
            in_specs=specs,
            out_specs=jax.tree.map(lambda _: pl.BlockSpec(memory_space=pltpu.VMEM), out_shape),
            scratch_shapes=[pltpu.VMEM(s, F32) for s in scratch],
            cost_estimate=pl.CostEstimate(flops=flops, bytes_accessed=1 << 16, transcendentals=0),
            compiler_params=pltpu.CompilerParams(vmem_limit_bytes=32 << 20),
        )(*args)

    return run


def pack_narrow(kirchhoff, adjoint, design, shape):
    x_fine, y_fine, z_fine = kirchhoff.shape
    low = pl.BlockSpec((x_fine, 8, z_fine), lambda i: (0, 0, 0))
    high = pl.BlockSpec((x_fine, 8, z_fine), lambda i: (0, y_fine // 8 - 1, 0))
    out = pl.BlockSpec(shape, lambda i: (0, 0))
    return pl.pallas_call(
        pack_kernel,
        grid=(1,),
        out_shape=[jax.ShapeDtypeStruct(shape, F32)] * 2,
        in_specs=[low, high, low, high, pl.BlockSpec(design.shape, lambda i: (0, 0, 0))],
        out_specs=[out, out],
    )(kirchhoff, kirchhoff, adjoint, adjoint, design)


def pack_wide(kirchhoff, adjoint, packed, shape):
    x_fine = kirchhoff.shape[0]
    low = pl.BlockSpec((1, *shape[1:]), lambda i: (0, 0, 0))
    high = pl.BlockSpec((1, *shape[1:]), lambda i: (x_fine - 1, 0, 0))
    out, unread = pl.BlockSpec(shape, lambda i: (0, 0, 0)), pl.BlockSpec(memory_space=pl.ANY)
    return pl.pallas_call(
        pack_wide_kernel,
        grid=(1,),
        out_shape=[jax.ShapeDtypeStruct(shape, F32)] * 2,
        in_specs=[low, high, low, high, unread, unread],
        out_specs=[out, out],
        cost_estimate=pl.CostEstimate(flops=1 << 30, bytes_accessed=1 << 16, transcendentals=0),
    )(kirchhoff, kirchhoff, adjoint, adjoint, *packed)


def swap(to_first, to_second, axis):
    count = lax.axis_size(axis)
    pairs = [[(i, i + 1) for i in range(start, count - 1, 2)] for start in (0, 1)]
    both = [[*p, *((j, i) for i, j in p)] for p in pairs]
    return lax.ppermute(to_first, axis, both[0]), lax.ppermute(to_second, axis, both[1])


def exchange(values, axis):
    return lax.all_to_all(values, axis, split_axis=0, concat_axis=0, tiled=True)


def exchange_rows(values, axis):
    rows, lanes = values.shape
    return exchange(values.reshape(rows, 1, lanes), axis).reshape(rows, lanes)


def per_device(kirchhoff, adjoint, penalty_slope, design, solid_mask, void_mask):
    wide, narrow = lax.axis_size("wide"), lax.axis_size("narrow")
    z_all, y_all = ZC * narrow, design.shape[2]
    x_fine = kirchhoff.shape[0]

    packed = (4 * x_fine + XC * RADIUS, y_all)
    packed = pack_narrow(kirchhoff, adjoint, design, packed)
    n_first, n_second = swap(*packed, "narrow")
    layers = (2, *kirchhoff.shape[1:])
    layers = pack_wide(kirchhoff, adjoint, packed, layers)
    x_first, x_second = swap(*layers, "wide")
    coarse = call(restrict_kernel, (YW * narrow, LANES))(
        kirchhoff, adjoint, penalty_slope, x_first, x_second, n_first, n_second
    )
    lines = call(design_kernel, (wide, 2 * LANES), flops=1 << 36)(design, solid_mask, void_mask, n_first, n_second)
    place = jnp.stack([lax.axis_index("wide"), lax.axis_index("narrow")]).astype(jnp.int32)
    lines, coarse, place = lax.optimization_barrier((lines, coarse, place))
    coarse = exchange(coarse, "narrow")
    sent = jnp.concatenate([lines[:, :LANES], lines[:, LANES:] * coarse], axis=1)

    got = exchange_rows(sent, "wide")

    def weigh(*refs):
        weigh_kernel(z_all, y_all, *refs)

    sent = call(weigh, (wide, 2 * LANES), smem=(0,))(place, got)
    got = exchange_rows(sent, "wide")
    packed = (3 * wide // 4, LANES)
    first, second = swap(*call(pack_planes_kernel, (packed, packed))(got), "narrow")
    projected = call(density_kernel, design.shape)(got, solid_mask, void_mask)
    sens = call(sens_kernel, design.shape)(first, got, second, solid_mask, void_mask)
    return projected, sens


def solution(mesh):
    fields = P("wide", "narrow", None)
    cells = P("narrow", "wide", None)
    return jax.shard_map(
        per_device,
        mesh=mesh,
        in_specs=(fields, fields, fields, cells, cells, cells),
        out_specs=(cells, cells),
        check_vma=False,
    )
```
